256 devices in a mesh: lat: 16 (over x, y_lo, core), lon: 16 (over z, y_hi).
Axes of the slice: x: 4, y: 4 (y_hi: 2, y_lo: 2; y = y_hi * 2 + y_lo), z: 8, core: 2. Of those that a mesh axis runs over, the one named last changes fastest.
Arguments:
- tokens: bfloat16 [16, 32, 128, 1024], P('lat', 'lon'), may hold values from -80 to 80
- w_qkv: bfloat16 [1024, 3072], replicated, may hold values from -0.1875 to 0.1875
- w_out: bfloat16 [1024, 1024], replicated, may hold values from -0.1875 to 0.1875
- tele_ids: int32 [16, 32, 8], P('lat', 'lon'), may hold values from 0 to 31, as said below
Outputs:
- mixed: bfloat16 [16, 32, 128, 1024], P('lat', 'lon')
The draws below stay inside these ranges and needn't reach their ends.
Inputs may be any that keep to these rules, and one draw needn't show every extreme that they name: `tele_ids`: the 16 entries of one device's query tiles name exactly 1 tile columns of each lon device, lon device o holding the tile columns o * 2 to o * 2 + 1.
All inputs are finite; a program needn't handle non-finite values.
Results may differ from the reference program's by a relative error of at most 0.013.
The reference program's roundings to bfloat16 on the way count: a program that leaves them out, or rounds other values in their place, can miss the bound.
Values may be sent and summed in bfloat16 or wider, within the bound.
A program may use at most 128 MiB of HBM per device.

```python
import jax
import jax.numpy as jnp
from jax import lax

D = 1024
H = 16
HD = 64
BLOCK = 128
TELE = 8
TL = 1
TO = 2
NT_LAT = 16
NT_LON = 32
N_LAT = 16
N_LON = 16


def draw_tokens(key, part):
    full_shape = (NT_LAT, NT_LON, BLOCK, D)
    base_key = jax.random.fold_in(jax.random.fold_in(key, 3), 0)
    values = jnp.clip(jax.random.normal(base_key, full_shape, jnp.float32), -5.0, 5.0)
    return values.astype(jnp.bfloat16)


def owner_order(sub_key):
    return jax.random.permutation(sub_key, N_LON)


def draw_tele_ids(key, part):
    device_count = N_LAT * N_LON
    request_count = TL * TO * TELE
    owner_key, order_key, column_key = jax.random.split(jax.random.fold_in(key, 17), 3)
    owner_perms = jax.vmap(owner_order)(jax.random.split(owner_key, device_count))
    cycled = jnp.arange(request_count, dtype=jnp.int32) % N_LON
    owners = jnp.take(owner_perms, cycled, axis=1)

    def slot_order(sub_key):
        return jax.random.permutation(sub_key, request_count)
    orders = jax.vmap(slot_order)(jax.random.split(order_key, device_count))
    owners = jnp.take_along_axis(owners, orders, axis=1)
    columns = jax.random.randint(column_key, (device_count, request_count), 0, TO, jnp.int32)
    picks = (owners * TO + columns).astype(jnp.int32)
    picks = picks.reshape(N_LAT, N_LON, TL, TO, TELE).transpose(0, 2, 1, 3, 4)
    return picks.reshape(NT_LAT, NT_LON, TELE)


def scatter_about(rng, shape, spread, bound, kind=jnp.bfloat16):
    values = spread * jax.random.normal(rng, shape, jnp.float32)
    return jnp.clip(values, min=-bound, max=bound).astype(kind)


def setup_inputs(seed: int = 0) -> dict:
    streams_of = jax.random.split(jax.random.key(seed), 5)
    tokens = draw_tokens(jax.random.fold_in(streams_of[4], 71), 0)
    w_qkv = scatter_about(streams_of[1], (D, 3 * D), D ** -0.5, 0.1875)
    w_out = scatter_about(streams_of[2], (D, D), D ** -0.5, 0.1875)
    tele_ids = draw_tele_ids(jax.random.fold_in(streams_of[4], 71), 0)
    return {"tokens": tokens, "w_qkv": w_qkv, "w_out": w_out, "tele_ids": tele_ids}


def attend(query, pairs, usable):
    tile_count = query.shape[0]
    key_count = pairs.shape[1]
    model_width = query.shape[2]
    group_width = 2 * HD

    def one_group(group_index):
        column_start = (group_index * group_width).astype(jnp.int32)
        queries = lax.dynamic_slice_in_dim(query, column_start, group_width, 2)
        queries = queries.reshape(tile_count, BLOCK, 2, HD).astype(jnp.float32)
        key_part = lax.dynamic_slice_in_dim(pairs, column_start, group_width, 2)
        key_part = key_part.reshape(tile_count, key_count, 2, HD).astype(jnp.float32)
        value_part = lax.dynamic_slice_in_dim(pairs, model_width + column_start, group_width, 2)
        value_part = value_part.reshape(tile_count, key_count, 2, HD).astype(jnp.float32)
        scores = jnp.einsum("tqhd,tkhd->thqk", queries, key_part) * (HD ** -0.5)
        scores = jnp.where(usable[:, None, None, :], scores, -1e30)
        peak = jnp.max(scores, axis=-1, keepdims=True)
        expos = jnp.exp(scores - peak)
        weights = (expos / jnp.sum(expos, axis=-1, keepdims=True)).astype(jnp.bfloat16)
        summed = jnp.einsum("thqk,tkhd->tqhd", weights.astype(jnp.float32), value_part)
        return summed.astype(jnp.bfloat16).reshape(tile_count, BLOCK, group_width)

    outputs = lax.map(one_group, jnp.arange(H // 2, dtype=jnp.int32))
    return outputs.transpose(1, 2, 0, 3).reshape(tile_count, BLOCK, model_width)


def reference(tokens, w_qkv, w_out, tele_ids):
    model_width = tokens.shape[3]
    flat_tokens = tokens.reshape(-1, model_width)
    projected = jnp.dot(flat_tokens, w_qkv, preferred_element_type=jnp.float32).astype(jnp.bfloat16)
    projected = projected.reshape(NT_LAT, NT_LON, BLOCK, 3 * model_width)
    queries_all = projected[..., :model_width]
    pairs_all = projected[..., model_width:]
    padded = jnp.pad(pairs_all, ((1, 1), (0, 0), (0, 0), (0, 0)))

    def one_row(row_index):
        query_row = lax.dynamic_index_in_dim(queries_all, row_index, 0, keepdims=False)
        blocks = []
        flags = []
        for lat_step in range(3):
            padded_row = lax.dynamic_index_in_dim(padded, row_index + lat_step, 0, keepdims=False)
            global_row = row_index + lat_step - 1
            inside = (global_row >= 0) & (global_row < NT_LAT)
            for lon_step in (-1, 0, 1):
                blocks.append(jnp.roll(padded_row, -lon_step, axis=0))
                flags.append(jnp.full((BLOCK,), inside))
        own_row = lax.dynamic_index_in_dim(pairs_all, row_index, 0, keepdims=False)
        picks = lax.dynamic_index_in_dim(tele_ids, row_index, 0, keepdims=False)
        far_tiles = jnp.take(own_row, picks.astype(jnp.int32), axis=0)
        near_tiles = jnp.stack(blocks, axis=1)
        pairs = jnp.concatenate([near_tiles, far_tiles], axis=1)
        pairs = pairs.reshape(NT_LON, (9 + TELE) * BLOCK, 2 * model_width)
        usable = jnp.concatenate(flags + [jnp.ones((TELE * BLOCK,), jnp.bool_)])
        usable = jnp.broadcast_to(usable[None, :], (NT_LON, usable.shape[0]))
        return attend(query_row, pairs, usable)

    attended = lax.map(one_row, jnp.arange(NT_LAT, dtype=jnp.int32))
    mixed = jnp.dot(attended.reshape(-1, model_width), w_out, preferred_element_type=jnp.float32)
    return mixed.astype(jnp.bfloat16).reshape(tokens.shape)
```

```python
import functools

import jax
import jax.numpy as jnp
from jax import lax
from jax.experimental import pallas as pl
from jax.experimental.pallas import tpu as pltpu
from jax.sharding import PartitionSpec as P

MESH = pl.DeviceIdType.MESH
BF = jnp.bfloat16
F32 = jnp.float32
H = 16
HD = 64
BLOCK = 128
PAIRS = H // 2
SENDS = 36


def nt_dot(a, b):
    return lax.dot_general(a, b, (((1,), (1,)), ((), ())), preferred_element_type=F32)


def nn_dot(a, b):
    return jnp.dot(a, b, preferred_element_type=F32)


def layer_kernel(
    comm,
    compute,
    ids,
    tok,
    wqkv,
    wout,
    out,
    g,
    nb,
    wq,
    wvt,
    wo,
    x,
    kn,
    vn,
    kt,
    vt,
    qmt,
    ms,
    ls,
    acc,
    att,
    send_sem,
    g_sem,
    n_sem,
    load_sem,
):
    n_lat, n_lon = lax.axis_size("lat"), lax.axis_size("lon")
    n_z = n_lon // 2
    width = wo.shape[0]
    lat, lon = lax.axis_index("lat"), lax.axis_index("lon")
    z, y_hi = lon // 2, lon % 2
    core = lat % 2
    sign = 1 - 2 * core

    def at(step, line):
        return lax.rem(z + step + n_z, n_z) * 2 + (y_hi if line == 0 else 1 - y_hi)

    partner = at(0, 1)
    lat_chip = lat + sign
    lat_off = lax.rem(lat + n_lat - sign, n_lat)
    lon_left, lon_right = lax.rem(lon + n_lon - 1, n_lon), lax.rem(lon + 1, n_lon)
    off_inside = jnp.where(core == 0, lat > 0, lat < n_lat - 1)

    loads = [
        pltpu.make_async_copy(tok, g.at[lon], load_sem.at[0]),
        pltpu.make_async_copy(wqkv, wq, load_sem.at[1]),
        pltpu.make_async_copy(wout, wo, load_sem.at[2]),
    ]
    for load in loads:
        load.start()

    sends = []

    def send(src, dst, sem, dev):
        if comm:
            copy = pltpu.make_async_remote_copy(
                src_ref=src,
                dst_ref=dst,
                send_sem=send_sem.at[len(sends)],
                recv_sem=sem,
                device_id=dev,
                device_id_type=MESH,
            )
            copy.start()
            sends.append(copy)

    def arrived(ref, sem):
        if comm:
            pltpu.make_async_remote_copy(
                src_ref=ref,
                dst_ref=ref,
                send_sem=send_sem.at[0],
                recv_sem=sem,
                device_id=(lat, partner),
                device_id_type=MESH,
            ).wait_recv()

    def send_g(owner, col, dev):
        send(g.at[owner, col], g.at[owner, col], g_sem.at[owner, col], dev)

    def wait_g(owner, col):
        arrived(g.at[owner, col], g_sem.at[owner, col])

    if comm:
        barrier = pltpu.get_barrier_semaphore()
        friends = [
            (lat, at(1, 0)),
            (lat, at(-1, 0)),
            (lat, partner),
            (lat_chip, lon),
            (lat_off, lon),
            (lat_off, lon_left),
            (lat_off, lon_right),
        ]
        for friend in friends:
            pl.semaphore_signal(barrier, inc=1, device_id=friend, device_id_type=MESH)
        pl.semaphore_wait(barrier, len(friends))

    up, down = (lat, at(1, 0)), (lat, at(-1, 0))
    across = (lat, partner)

    def send_own(col, dev):
        send(tok.at[col], g.at[lon, col], g_sem.at[lon, col], dev)

    send_own(0, across)
    send_own(1, up)
    send_own(1, down)
    send_own(0, up)
    send_own(0, down)
    send(tok, nb.at[0, pl.ds(1, 2)], n_sem.at[0, 0], (lat_chip, lon))
    send(tok, nb.at[1, pl.ds(1, 2)], n_sem.at[1, 0], (lat_off, lon))
    send(tok.at[0], nb.at[1, 3], n_sem.at[1, 2], (lat_off, lon_left))
    send(tok.at[1], nb.at[1, 0], n_sem.at[1, 1], (lat_off, lon_right))
    send_own(1, across)

    def lookup(owner):
        col = jnp.int32(0)
        which = jnp.int32(0)
        for entry in range(16):
            value = ids[entry]
            hit = lax.shift_right_logical(value, 1) == owner
            col = jnp.where(hit, value & 1, col)
            which = jnp.where(hit, jnp.int32(entry // 8), which)
        return col, which

    def project(source, k_dst, v_dst):
        @pl.loop(0, width // 256)
        def _(step):
            cols = pl.ds(pl.multiple_of(step * 256, 256), 256)
            k_cols = pl.ds(pl.multiple_of(width + step * 256, 256), 256)
            k_dst[:, cols] = nn_dot(source[...], wq[:, k_cols]).astype(BF)
            v_dst[cols, :] = nt_dot(wvt[cols, :], source[...]).astype(BF)

    def pair_cols(pair):
        return pl.ds(pl.multiple_of(pair * 128, 128), 128)

    def merge(pair, j, scores, values, first):
        peak = jnp.max(scores[0], axis=0, keepdims=True)
        for s in scores[1:]:
            peak = jnp.maximum(peak, jnp.max(s, axis=0, keepdims=True))
        if not first:
            before = ms[j, pair]
            peak = jnp.maximum(peak, before)
        total = None
        summed = None
        for s, v in zip(scores, values):
            expos = jnp.exp(s - peak)
            part = jnp.sum(expos, axis=0, keepdims=True)
            prod = nn_dot(v, expos.astype(BF))
            total = part if total is None else total + part
            summed = prod if summed is None else summed + prod
        even, odd = summed[:HD, :BLOCK], summed[HD:, BLOCK:]
        if not first:
            decay = jnp.exp(before - peak)
            total = total + ls[j, pair] * decay
            even = even + acc[j, pair, 0] * decay[:, :BLOCK]
            odd = odd + acc[j, pair, 1] * decay[:, BLOCK:]
        ms[j, pair] = peak
        ls[j, pair] = total
        acc[j, pair, 0] = even
        acc[j, pair, 1] = odd

    def near(keys_of, first):
        @pl.loop(0, PAIRS)
        def _(pair):
            cols = pair_cols(pair)
            for j in range(2):
                queries = qmt[j, pair]
                scores, values = [], []
                for row, start, size in keys_of(j):
                    scores.append(nn_dot(kn[row, pl.ds(start, size), cols], queries))
                    values.append(vn[row, cols, pl.ds(start, size)])
                merge(pair, j, scores, values, first)

    def far(owners):
        count = len(owners)
        whiches = []
        for i, owner in enumerate(owners):
            col, which = lookup(owner)
            whiches.append(which)
            x[i * BLOCK : (i + 1) * BLOCK] = jnp.where(col == 1, g[owner, 1], g[owner, 0])
        rows = pl.ds(0, count * BLOCK)
        project(x.at[rows], kt.at[rows], vt.at[:, rows])

        @pl.loop(0, PAIRS)
        def _(pair):
            cols = pair_cols(pair)
            scores = []
            peaks = []
            for i in range(count):
                s = nn_dot(kt[i * BLOCK : (i + 1) * BLOCK, cols], qmt[whiches[i], pair])
                scores.append(s)
                peaks.append(jnp.max(s, axis=0, keepdims=True))
            before = [ms[j, pair] for j in range(2)]
            now = []
            for j in range(2):
                peak = before[j]
                for i in range(count):
                    peak = jnp.maximum(peak, jnp.where(whiches[i] == j, peaks[i], before[j]))
                now.append(peak)
            decay = [jnp.exp(before[j] - now[j]) for j in range(2)]
            totals = [ls[j, pair] * decay[j] for j in range(2)]
            evens = [acc[j, pair, 0] * decay[j][:, :BLOCK] for j in range(2)]
            odds = [acc[j, pair, 1] * decay[j][:, BLOCK:] for j in range(2)]
            for i in range(count):
                expos = jnp.exp(scores[i] - jnp.where(whiches[i] == 0, now[0], now[1]))
                part = jnp.sum(expos, axis=0, keepdims=True)
                prod = nn_dot(vt[cols, i * BLOCK : (i + 1) * BLOCK], expos.astype(BF))
                even, odd = prod[:HD, :BLOCK], prod[HD:, BLOCK:]
                for j in range(2):
                    mine = whiches[i] == j
                    totals[j] = totals[j] + jnp.where(mine, part, 0.0)
                    evens[j] = evens[j] + jnp.where(mine, even, 0.0)
                    odds[j] = odds[j] + jnp.where(mine, odd, 0.0)
            for j in range(2):
                ms[j, pair] = now[j]
                ls[j, pair] = totals[j]
                acc[j, pair, 0] = evens[j]
                acc[j, pair, 1] = odds[j]

    def own_projection():
        own = g.at[lon]

        @pl.loop(0, width // 128)
        def _(step):
            cols = pl.ds(pl.multiple_of(step * 128, 128), 128)
            v_cols = pl.ds(pl.multiple_of(2 * width + step * 128, 128), 128)
            wvt[cols, :] = wq[:, v_cols].T

        @pl.loop(0, width // 256)
        def _(step):
            cols = pl.ds(pl.multiple_of(step * 256, 256), 256)
            tokens = own[...].reshape(2 * BLOCK, width)
            queries = nn_dot(tokens, wq[:, cols]).astype(BF).astype(F32) * HD**-0.5
            row = lax.broadcasted_iota(jnp.int32, (BLOCK, BLOCK), 0)
            for j in range(2):
                for half in range(2):
                    block = queries[j * BLOCK : (j + 1) * BLOCK, half * 128 : (half + 1) * 128].T
                    even = jnp.where(row < HD, block, 0.0)
                    odd = jnp.where(row < HD, 0.0, block)
                    qmt[j, step * 2 + half] = jnp.concatenate([even, odd], axis=1).astype(BF)
        x[: 2 * BLOCK] = own[...].reshape(2 * BLOCK, width)
        project(x.at[pl.ds(0, 256)], kn.at[0, pl.ds(128, 256)], vn.at[0, :, pl.ds(128, 256)])

    def finish():
        @pl.loop(0, PAIRS)
        def _(pair):
            cols = pair_cols(pair)
            for j in range(2):
                total = ls[j, pair]
                even = acc[j, pair, 0] / total[:, :BLOCK]
                odd = acc[j, pair, 1] / total[:, BLOCK:]
                att[j * BLOCK : (j + 1) * BLOCK, cols] = jnp.concatenate([even, odd], axis=0).T.astype(BF)

        @pl.loop(0, width // 256)
        def _(step):
            cols = pl.ds(pl.multiple_of(step * 256, 256), 256)
            out[:, cols] = nn_dot(att[...], wo[:, cols]).astype(BF)

    for load in loads:
        load.wait()
    if compute:
        own_projection()

    wait_g(partner, 0)
    send_g(partner, 0, up)
    send_g(partner, 0, down)

    def relay(step):
        for line, col in ((0, 1), (0, 0), (1, 0)):
            low, high = at(-step, line), at(step, line)
            wait_g(low, col)
            wait_g(high, col)
            if step < n_z // 2 - 1:
                send_g(low, col, up)
                send_g(high, col, down)
            else:
                last = lax.rem(z + n_z - step * sign, n_z) * 2 + (y_hi if line == 0 else 1 - y_hi)
                send_g(last, col, (lat, lax.rem(z + n_z + sign, n_z) * 2 + y_hi))
            if line == 0 and col == 1:
                send_g(low, 1, across)
                send_g(high, 1, across)

    arrived(nb.at[0, pl.ds(1, 2)], n_sem.at[0, 0])
    if compute:
        x[: 2 * BLOCK] = nb[0, 1:3].reshape(2 * BLOCK, width)
        project(x.at[pl.ds(0, 256)], kn.at[1, pl.ds(128, 256)], vn.at[1, :, pl.ds(128, 256)])
        near(lambda j: ((0, 128, 256), (1, 128, 256)), True)

    relay(1)

    arrived(nb.at[1, pl.ds(1, 2)], n_sem.at[1, 0])
    arrived(nb.at[1, 0], n_sem.at[1, 1])
    arrived(nb.at[1, 3], n_sem.at[1, 2])
    if compute:
        @pl.when(off_inside)
        def _():
            x[...] = nb[1].reshape(4 * BLOCK, width)
            project(x, kn.at[2], vn.at[2])
            near(lambda j: ((2, j * BLOCK, 3 * BLOCK),), False)

    wait_g(partner, 1)
    wait_g(at(-1, 1), 1)
    wait_g(at(1, 1), 1)
    send(g.at[lon_left, 1], nb.at[0, 0], n_sem.at[0, 1], (lat_chip, lon))
    send(g.at[lon_right, 0], nb.at[0, 3], n_sem.at[0, 2], (lat_chip, lon))
    if compute:
        far([at(-1, 0), at(1, 0), at(-1, 1), at(1, 1)])

    relay(2)

    arrived(nb.at[0, 0], n_sem.at[0, 1])
    arrived(nb.at[0, 3], n_sem.at[0, 2])
    if compute:
        x[0:128] = g[lon_left, 1]
        x[128:256] = g[lon_right, 0]
        x[256:384] = nb[0, 0]
        x[384:512] = nb[0, 3]
        project(x, kt, vt)
        for i, (row, start) in enumerate(((0, 0), (0, 384), (1, 0), (1, 384))):
            kn[row, start : start + BLOCK] = kt[i * BLOCK : (i + 1) * BLOCK]
            vn[row, :, start : start + BLOCK] = vt[:, i * BLOCK : (i + 1) * BLOCK]
        near(lambda j: ((0, j * 384, BLOCK), (1, j * 384, BLOCK)), False)
        far([lon, partner])

    wait_g(at(-2, 1), 1)
    wait_g(at(2, 1), 1)
    if compute:
        far([at(-2, 0), at(2, 0), at(-2, 1), at(2, 1)])

    relay(3)

    wait_g(at(-3, 1), 1)
    wait_g(at(3, 1), 1)
    if compute:
        far([at(-3, 0), at(3, 0), at(-3, 1), at(3, 1)])

    wait_g(at(4, 0), 1)
    send_g(at(4, 0), 1, across)
    wait_g(at(4, 0), 0)
    wait_g(at(4, 1), 0)
    wait_g(at(4, 1), 1)
    if compute:
        far([at(4, 0), at(4, 1)])
        finish()
    else:
        out[...] = g[lon].reshape(out.shape)
    for copy in sends:
        copy.wait_send()


def on_device(tokens, w_qkv, w_out, tele_ids, comm=True, compute=True):
    shape = tokens.shape
    width = shape[3]
    tokens = tokens.reshape(2, BLOCK, width)
    n_lon = lax.axis_size("lon")
    anywhere = pl.BlockSpec(memory_space=pl.ANY)
    mixed = pl.pallas_call(
        functools.partial(layer_kernel, comm, compute),
        out_shape=jax.ShapeDtypeStruct((2 * BLOCK, width), BF),
        in_specs=[pl.BlockSpec(memory_space=pltpu.SMEM), anywhere, anywhere, anywhere],
        out_specs=pl.BlockSpec(memory_space=pltpu.VMEM),
        scratch_shapes=[
            pltpu.VMEM((n_lon, 2, BLOCK, width), BF),
            pltpu.VMEM((2, 4, BLOCK, width), BF),
            pltpu.VMEM((width, 3 * width), BF),
            pltpu.VMEM((width, width), BF),
            pltpu.VMEM((width, width), BF),
            pltpu.VMEM((4 * BLOCK, width), BF),
            pltpu.VMEM((3, 4 * BLOCK, width), BF),
            pltpu.VMEM((3, width, 4 * BLOCK), BF),
            pltpu.VMEM((4 * BLOCK, width), BF),
            pltpu.VMEM((width, 4 * BLOCK), BF),
            pltpu.VMEM((2, PAIRS, 2 * HD, 2 * BLOCK), BF),
            pltpu.VMEM((2, PAIRS, 1, 2 * BLOCK), F32),
            pltpu.VMEM((2, PAIRS, 1, 2 * BLOCK), F32),
            pltpu.VMEM((2, PAIRS, 2, HD, BLOCK), F32),
            pltpu.VMEM((2 * BLOCK, width), BF),
            pltpu.SemaphoreType.DMA((SENDS,)),
            pltpu.SemaphoreType.DMA((n_lon, 2)),
            pltpu.SemaphoreType.DMA((2, 3)),
            pltpu.SemaphoreType.DMA((3,)),
        ],
        compiler_params=pltpu.CompilerParams(
            collective_id=0 if comm else None, has_side_effects=True, vmem_limit_bytes=60 * 1024 * 1024
        ),
        name="layer",
    )(tele_ids.reshape(-1), tokens, w_qkv, w_out)
    return mixed.reshape(shape)


def solution(mesh):
    return jax.shard_map(
        on_device,
        mesh=mesh,
        in_specs=(P("lat", "lon", None, None), P(), P(), P("lat", "lon", None)),
        out_specs=P("lat", "lon", None, None),
        check_vma=False,
    )
```

```python
import functools

import jax
import jax.numpy as jnp
from jax import lax
from jax.experimental import pallas as pl
from jax.experimental.pallas import tpu as pltpu
from jax.sharding import PartitionSpec as P

MESH = pl.DeviceIdType.MESH
BF = jnp.bfloat16
F32 = jnp.float32
H = 16
HD = 64
BLOCK = 128
PAIRS = H // 2
SENDS = 40
TELE = 8
UNROLL = 2


def nt_dot(a, b):
    return lax.dot_general(a, b, (((1,), (1,)), ((), ())), preferred_element_type=F32)


def nn_dot(a, b):
    return jnp.dot(a, b, preferred_element_type=F32)


def layer_kernel(
    comm,
    compute,
    ids,
    ids_hbm,
    tok,
    wqkv,
    wout,
    out,
    g,
    nb,
    pick,
    picked,
    wq,
    wvt,
    wo,
    x,
    kn,
    vn,
    kt,
    vt,
    qmt,
    ms,
    ls,
    acc,
    att,
    sb0,
    sb1,
    pk0,
    pk1,
    ids_in,
    ids_across,
    send_sem,
    g_sem,
    n_sem,
    chip_sem,
    pick_sem,
    ids_sem,
    load_sem,
):
    n_lat, n_lon = lax.axis_size("lat"), lax.axis_size("lon")
    n_z = n_lon // 2
    width = wo.shape[0]
    lat, lon = lax.axis_index("lat"), lax.axis_index("lon")
    z, y_hi = lon // 2, lon % 2
    core = lat % 2
    sign = 1 - 2 * core

    def at(step, line):
        return lax.rem(z + step + n_z, n_z) * 2 + (y_hi if line == 0 else 1 - y_hi)

    partner = at(0, 1)
    sb, pk = (sb0, sb1), (pk0, pk1)
    lat_chip = lat + sign
    lat_off = lax.rem(lat + n_lat - sign, n_lat)
    lon_left, lon_right = lax.rem(lon + n_lon - 1, n_lon), lax.rem(lon + 1, n_lon)
    off_inside = jnp.where(core == 0, lat > 0, lat < n_lat - 1)

    loads = [
        pltpu.make_async_copy(tok, g.at[lon], load_sem.at[0]),
        pltpu.make_async_copy(wqkv, wq, load_sem.at[1]),
        pltpu.make_async_copy(wout, wo, load_sem.at[2]),
    ]
    for load in loads:
        load.start()

    sends = []

    def send(src, dst, sem, dev):
        if comm:
            copy = pltpu.make_async_remote_copy(
                src_ref=src,
                dst_ref=dst,
                send_sem=send_sem.at[len(sends)],
                recv_sem=sem,
                device_id=dev,
                device_id_type=MESH,
            )
            copy.start()
            sends.append(copy)

    def arrived(ref, sem):
        if comm:
            pltpu.make_async_remote_copy(
                src_ref=ref,
                dst_ref=ref,
                send_sem=send_sem.at[0],
                recv_sem=sem,
                device_id=(lat, partner),
                device_id_type=MESH,
            ).wait_recv()

    def send_g(owner, col, dev):
        send(g.at[owner, col], g.at[owner, col], g_sem.at[owner, col], dev)

    def wait_g(owner, col):
        arrived(g.at[owner, col], g_sem.at[owner, col])

    if comm:
        barrier = pltpu.get_barrier_semaphore()
        friends = [
            (lat, at(1, 0)),
            (lat, at(-1, 0)),
            (lat, partner),
            (lat_chip, lon),
            (lat_off, lon),
            (lat_off, lon_left),
            (lat_off, lon_right),
        ]
        for friend in friends:
            pl.semaphore_signal(barrier, inc=1, device_id=friend, device_id_type=MESH)
        pl.semaphore_wait(barrier, len(friends))

    up, down = (lat, at(1, 0)), (lat, at(-1, 0))
    across = (lat, partner)

    def send_own(col, dev):
        send(tok.at[col], g.at[lon, col], g_sem.at[lon, col], dev)

    send(ids_hbm, ids_in, ids_sem.at[0], across)
    send_own(0, across)
    send_own(1, across)
    send_own(1, up)
    send_own(1, down)
    send_own(0, up)
    send_own(0, down)
    send(tok, nb.at[pl.ds(0, 2)], n_sem.at[0], (lat_off, lon))
    send(tok.at[1], nb.at[2], n_sem.at[1], (lat_off, lon_right))
    send(tok.at[0], nb.at[3], n_sem.at[2], (lat_off, lon_left))

    def lookup(owner, table=None):
        col = jnp.int32(0)
        which = jnp.int32(0)
        for entry in range(2 * TELE):
            value = ids[entry] if table is None else table[0, entry]
            hit = lax.shift_right_logical(value, 1) == owner
            col = jnp.where(hit, value & 1, col)
            which = jnp.where(hit, jnp.int32(entry // TELE), which)
        return col, which

    def project(source, k_dst, v_dst):
        @pl.loop(0, width // 256, unroll=UNROLL)
        def _(step):
            cols = pl.ds(pl.multiple_of(step * 256, 256), 256)
            k_cols = pl.ds(pl.multiple_of(width + step * 256, 256), 256)
            k_dst[:, cols] = nn_dot(source[...], wq[:, k_cols]).astype(BF)
            v_dst[cols, :] = nt_dot(wvt[cols, :], source[...]).astype(BF)

    def pair_cols(pair):
        return pl.ds(pl.multiple_of(pair * 128, 128), 128)

    def pipelined(score, finish_pair):
        score(0, 0)

        @pl.loop(0, PAIRS // 2)
        def _(step):
            score(2 * step + 1, 1)
            finish_pair(2 * step, 0)
            score(jnp.minimum(2 * step + 2, PAIRS - 1), 0)
            finish_pair(2 * step + 1, 1)

    def near(keys_of, first):
        sizes = [size for _, _, size in keys_of(0)]
        count = sum(sizes)

        def score(pair, slot):
            cols = pair_cols(pair)
            for j in range(2):
                queries = qmt[j, pair]
                offset = j * count
                peak = None
                for row, start, size in keys_of(j):
                    s = nn_dot(kn[row, pl.ds(start, size), cols], queries)
                    sb[slot][pl.ds(offset, size)] = s
                    top = jnp.max(s, axis=0, keepdims=True)
                    peak = top if peak is None else jnp.maximum(peak, top)
                    offset += size
                pk[slot][j] = peak

        def finish_pair(pair, slot):
            cols = pair_cols(pair)
            for j in range(2):
                peak = pk[slot][j]
                if not first:
                    before = ms[j, pair]
                    peak = jnp.maximum(peak, before)
                total = None
                summed = None
                offset = j * count
                for row, start, size in keys_of(j):
                    expos = jnp.exp(sb[slot][pl.ds(offset, size)] - peak)
                    part = jnp.sum(expos, axis=0, keepdims=True)
                    prod = nn_dot(vn[row, cols, pl.ds(start, size)], expos.astype(BF))
                    total = part if total is None else total + part
                    summed = prod if summed is None else summed + prod
                    offset += size
                even, odd = summed[:HD, :BLOCK], summed[HD:, BLOCK:]
                if not first:
                    decay = jnp.exp(before - peak)
                    total = total + ls[j, pair] * decay
                    even = even + acc[j, pair, 0] * decay[:, :BLOCK]
                    odd = odd + acc[j, pair, 1] * decay[:, BLOCK:]
                ms[j, pair] = peak
                ls[j, pair] = total
                acc[j, pair, 0] = even
                acc[j, pair, 1] = odd

        pipelined(score, finish_pair)

    def far(tiles, own=False):
        whiches = []
        for i, (owner, both, one) in enumerate(tiles):
            col, which = lookup(owner)
            whiches.append(which)
            rows = slice(i * BLOCK, (i + 1) * BLOCK)
            x[rows] = one[...] if both is None else jnp.where(col == 1, both[1], both[0])
        rows = pl.ds(0, len(tiles) * BLOCK)
        project(x.at[rows], kt.at[rows], vt.at[:, rows])
        if own:
            col, which = lookup(lon)
            last = slice(len(tiles) * BLOCK, (len(tiles) + 1) * BLOCK)
            whiches.append(which)
            kt[last] = jnp.where(col == 1, kn[0, BLOCK : 2 * BLOCK], kn[0, :BLOCK])
            vt[:, last] = jnp.where(col == 1, vn[0, :, BLOCK : 2 * BLOCK], vn[0, :, :BLOCK])
        count = len(whiches)
        keys = count * BLOCK

        def score(pair, slot):
            cols = pair_cols(pair)
            for i in range(count):
                s = nn_dot(kt[i * BLOCK : (i + 1) * BLOCK, cols], qmt[whiches[i], pair])
                sb[slot][i * BLOCK : (i + 1) * BLOCK] = s
                pk[slot][i] = jnp.max(s, axis=0, keepdims=True)

        def finish_pair(pair, slot):
            cols = pair_cols(pair)
            peaks = [pk[slot][i] for i in range(count)]
            before = [ms[j, pair] for j in range(2)]
            now = []
            for j in range(2):
                peak = before[j]
                for i in range(count):
                    peak = jnp.maximum(peak, jnp.where(whiches[i] == j, peaks[i], before[j]))
                now.append(peak)
            decay = [jnp.exp(before[j] - now[j]) for j in range(2)]
            totals = [ls[j, pair] * decay[j] for j in range(2)]
            weights = [[], []]
            for i in range(count):
                mine = whiches[i] == 0
                expos = jnp.exp(sb[slot][i * BLOCK : (i + 1) * BLOCK] - jnp.where(mine, now[0], now[1]))
                part = jnp.sum(expos, axis=0, keepdims=True)
                rounded = expos.astype(BF)
                none = jnp.zeros_like(rounded)
                totals[0] = totals[0] + jnp.where(mine, part, 0.0)
                totals[1] = totals[1] + jnp.where(mine, 0.0, part)
                weights[0].append(jnp.where(mine, rounded, none))
                weights[1].append(jnp.where(mine, none, rounded))
            for j in range(2):
                summed = nn_dot(vt[cols, :keys], jnp.concatenate(weights[j], axis=0))
                ms[j, pair] = now[j]
                ls[j, pair] = totals[j]
                acc[j, pair, 0] = acc[j, pair, 0] * decay[j][:, :BLOCK] + summed[:HD, :BLOCK]
                acc[j, pair, 1] = acc[j, pair, 1] * decay[j][:, BLOCK:] + summed[HD:, BLOCK:]

        pipelined(score, finish_pair)

    def own_projection():
        own = g.at[lon]

        @pl.loop(0, width // 128)
        def _(step):
            cols = pl.ds(pl.multiple_of(step * 128, 128), 128)
            v_cols = pl.ds(pl.multiple_of(2 * width + step * 128, 128), 128)
            wvt[cols, :] = wq[:, v_cols].T

        @pl.loop(0, width // 256)
        def _(step):
            cols = pl.ds(pl.multiple_of(step * 256, 256), 256)
            tokens = own[...].reshape(2 * BLOCK, width)
            queries = nn_dot(tokens, wq[:, cols]).astype(BF).astype(F32) * HD**-0.5
            row = lax.broadcasted_iota(jnp.int32, (BLOCK, BLOCK), 0)
            for j in range(2):
                for half in range(2):
                    block = queries[j * BLOCK : (j + 1) * BLOCK, half * 128 : (half + 1) * 128].T
                    even = jnp.where(row < HD, block, 0.0)
                    odd = jnp.where(row < HD, 0.0, block)
                    qmt[j, step * 2 + half] = jnp.concatenate([even, odd], axis=1).astype(BF)
        x[: 2 * BLOCK] = own[...].reshape(2 * BLOCK, width)
        project(x.at[pl.ds(0, 256)], kn.at[0, pl.ds(0, 256)], vn.at[0, :, pl.ds(0, 256)])

    def finish():
        @pl.loop(0, PAIRS)
        def _(pair):
            cols = pair_cols(pair)
            for j in range(2):
                total = ls[j, pair]
                even = acc[j, pair, 0] / total[:, :BLOCK]
                odd = acc[j, pair, 1] / total[:, BLOCK:]
                att[j * BLOCK : (j + 1) * BLOCK, cols] = jnp.concatenate([even, odd], axis=0).T.astype(BF)

        @pl.loop(0, width // 256)
        def _(step):
            cols = pl.ds(pl.multiple_of(step * 256, 256), 256)
            out[:, cols] = nn_dot(att[...], wo[:, cols]).astype(BF)

    def onward(owner, col, direction):
        send_g(owner, col, up if direction > 0 else down)

    def relay(step, col):
        wait_g(at(-step, 0), col)
        wait_g(at(step, 0), col)
        onward(at(-step, 0), col, 1)
        onward(at(step, 0), col, -1)

    def select(slot, owner):
        if comm:
            col, _ = lookup(owner, ids_across)
            pick[slot] = jnp.where(col == 1, g[owner, 1], g[owner, 0])

    def hand(slot):
        send(pick.at[slot], picked.at[slot], pick_sem.at[slot], across)

    def given(slot):
        arrived(picked.at[slot], pick_sem.at[slot])

    def both(step, line):
        owner = at(step, line)
        return owner, g.at[owner], None

    def single(step, slot):
        return at(step, 1), None, picked.at[slot]

    for load in loads:
        load.wait()
    if compute:
        own_projection()

    relay(1, 1)
    chip = (lat_chip, lon)
    send(kn.at[0, pl.ds(0, 256)], kn.at[1, pl.ds(0, 256)], chip_sem.at[0], chip)
    send(vn.at[0, :, pl.ds(0, 256)], vn.at[1, :, pl.ds(0, 256)], chip_sem.at[1], chip)
    if comm:
        arrived(ids_in, ids_sem.at[0])
        table = pltpu.make_async_copy(ids_in, ids_across, ids_sem.at[1])
        table.start()
        table.wait()
    relay(1, 0)
    arrived(kn.at[1, pl.ds(0, 256)], chip_sem.at[0])
    arrived(vn.at[1, :, pl.ds(0, 256)], chip_sem.at[1])
    if compute:
        near(lambda j: ((0, 0, 256), (1, 0, 256)), True)

    wait_g(partner, 0)
    wait_g(partner, 1)
    turn = 1 - 2 * y_hi
    ahead = (lat, lax.rem(z + turn + n_z, n_z) * 2 + y_hi)
    behind = (lat, lax.rem(z - turn + n_z, n_z) * 2 + y_hi)
    send_g(partner, 1 - y_hi, ahead)
    if compute:
        far([both(0, 1), both(-1, 0), both(1, 0)], own=True)

    relay(2, 1)
    relay(2, 0)
    select(0, at(-2, 0))
    select(1, at(2, 0))
    wait_g(lax.rem(z - turn + n_z, n_z) * 2 + 1 - y_hi, 1 - y_hi)
    if compute:
        x[0:128] = g[lon_left, 1]
        x[128:256] = g[lon_right, 0]
        project(x.at[pl.ds(0, 256)], kn.at[0, pl.ds(256, 256)], vn.at[0, :, pl.ds(256, 256)])
    hand(0)
    hand(1)
    send(kn.at[0, pl.ds(256, 256)], kn.at[1, pl.ds(256, 256)], chip_sem.at[2], chip)
    send(vn.at[0, :, pl.ds(256, 256)], vn.at[1, :, pl.ds(256, 256)], chip_sem.at[3], chip)

    arrived(nb.at[pl.ds(0, 2)], n_sem.at[0])
    arrived(nb.at[2], n_sem.at[1])
    arrived(nb.at[3], n_sem.at[2])
    if compute:
        @pl.when(off_inside)
        def _():
            project(nb.reshape(4 * BLOCK, width), kn.at[2], vn.at[2])
            near(lambda j: ((2, 0, 256), (2, 256 + j * BLOCK, BLOCK)), False)

    wait_g(at(-3, 0), 1)
    wait_g(at(3, 0), 1)
    wait_g(at(-3, 0), 0)
    wait_g(at(3, 0), 0)
    last = lax.rem(z + n_z - 3 * sign, n_z) * 2 + y_hi
    beyond = (lat, lax.rem(z + n_z + sign, n_z) * 2 + y_hi)
    send_g(last, 1, beyond)
    send_g(last, 0, beyond)
    select(2, at(-3, 0))
    select(3, at(3, 0))
    send_g(partner, 1 - y_hi, behind)
    send_g(partner, y_hi, ahead)
    send_g(partner, y_hi, behind)
    hand(2)
    hand(3)

    arrived(kn.at[1, pl.ds(256, 256)], chip_sem.at[2])
    arrived(vn.at[1, :, pl.ds(256, 256)], chip_sem.at[3])
    if compute:
        near(lambda j: ((0, 256 + j * BLOCK, BLOCK), (1, 256 + j * BLOCK, BLOCK)), False)

    given(0)
    given(1)
    if compute:
        far([both(-2, 0), both(2, 0), single(-2, 0), single(2, 1)])

    wait_g(at(4, 0), 1)
    wait_g(at(4, 0), 0)
    select(4, at(4, 0))
    hand(4)
    if compute:
        far([both(-3, 0), both(3, 0), both(4, 0)])

    given(2)
    given(3)
    wait_g(lax.rem(z + turn + n_z, n_z) * 2 + 1 - y_hi, 1 - y_hi)
    wait_g(at(-1, 1), y_hi)
    wait_g(at(1, 1), y_hi)
    if compute:
        far([both(-1, 1), both(1, 1), single(-3, 2), single(3, 3)])
    given(4)
    if compute:
        far([single(4, 4)])
        finish()
    else:
        out[...] = g[lon].reshape(out.shape)
    for copy in sends:
        copy.wait_send()


def on_device(tokens, w_qkv, w_out, tele_ids, comm=True, compute=True):
    shape = tokens.shape
    width = shape[3]
    tokens = tokens.reshape(2, BLOCK, width)
    n_lon = lax.axis_size("lon")
    anywhere = pl.BlockSpec(memory_space=pl.ANY)
    mixed = pl.pallas_call(
        functools.partial(layer_kernel, comm, compute),
        out_shape=jax.ShapeDtypeStruct((2 * BLOCK, width), BF),
        in_specs=[pl.BlockSpec(memory_space=pltpu.SMEM)] + [anywhere] * 4,
        out_specs=pl.BlockSpec(memory_space=pltpu.VMEM),
        scratch_shapes=[
            pltpu.VMEM((n_lon, 2, BLOCK, width), BF),
            pltpu.VMEM((4, BLOCK, width), BF),
            pltpu.VMEM((5, BLOCK, width), BF),
            pltpu.VMEM((5, BLOCK, width), BF),
            pltpu.VMEM((width, 3 * width), BF),
            pltpu.VMEM((width, width), BF),
            pltpu.VMEM((width, width), BF),
            pltpu.VMEM((4 * BLOCK, width), BF),
            pltpu.VMEM((3, 4 * BLOCK, width), BF),
            pltpu.VMEM((3, width, 4 * BLOCK), BF),
            pltpu.VMEM((4 * BLOCK, width), BF),
            pltpu.VMEM((width, 4 * BLOCK), BF),
            pltpu.VMEM((2, PAIRS, 2 * HD, 2 * BLOCK), BF),
            pltpu.VMEM((2, PAIRS, 1, 2 * BLOCK), F32),
            pltpu.VMEM((2, PAIRS, 1, 2 * BLOCK), F32),
            pltpu.VMEM((2, PAIRS, 2, HD, BLOCK), F32),
            pltpu.VMEM((2 * BLOCK, width), BF),
            pltpu.VMEM((8 * BLOCK, 2 * BLOCK), F32),
            pltpu.VMEM((8 * BLOCK, 2 * BLOCK), F32),
            pltpu.VMEM((4, 1, 2 * BLOCK), F32),
            pltpu.VMEM((4, 1, 2 * BLOCK), F32),
            pltpu.VMEM((1, 2 * TELE), jnp.int32),
            pltpu.SMEM((1, 2 * TELE), jnp.int32),
            pltpu.SemaphoreType.DMA((SENDS,)),
            pltpu.SemaphoreType.DMA((n_lon, 2)),
            pltpu.SemaphoreType.DMA((3,)),
            pltpu.SemaphoreType.DMA((4,)),
            pltpu.SemaphoreType.DMA((5,)),
            pltpu.SemaphoreType.DMA((2,)),
            pltpu.SemaphoreType.DMA((3,)),
        ],
        compiler_params=pltpu.CompilerParams(
            collective_id=0 if comm else None, has_side_effects=True, vmem_limit_bytes=60 * 1024 * 1024
        ),
        name="layer",
    )(tele_ids.reshape(-1), tele_ids.reshape(1, -1), tokens, w_qkv, w_out)
    return mixed.reshape(shape)


def solution(mesh):
    return jax.shard_map(
        on_device,
        mesh=mesh,
        in_specs=(P("lat", "lon", None, None), P(), P(), P("lat", "lon", None)),
        out_specs=P("lat", "lon", None, None),
        check_vma=False,
    )
```

```python
import functools

import jax
import jax.numpy as jnp
from jax import lax
from jax.experimental import pallas as pl
from jax.experimental.pallas import tpu as pltpu
from jax.sharding import PartitionSpec as P

MESH = pl.DeviceIdType.MESH
BF = jnp.bfloat16
F32 = jnp.float32
H = 16
HD = 64
BLOCK = 128
PAIRS = H // 2
SENDS = 40
TELE = 8
UNROLL = 2


def nt_dot(a, b):
    return lax.dot_general(a, b, (((1,), (1,)), ((), ())), preferred_element_type=F32)


def nn_dot(a, b):
    return jnp.dot(a, b, preferred_element_type=F32)


def layer_kernel(
    comm,
    compute,
    ids,
    ids_hbm,
    tok,
    wqkv,
    out,
    g,
    nb,
    pick,
    picked,
    wq,
    wvt,
    x,
    kn,
    vn,
    kt,
    vt,
    qmt,
    ms,
    ls,
    acc,
    sb0,
    sb1,
    pk0,
    pk1,
    ids_in,
    ids_across,
    send_sem,
    g_sem,
    n_sem,
    chip_sem,
    pick_sem,
    ids_sem,
    load_sem,
):
    n_lat, n_lon = lax.axis_size("lat"), lax.axis_size("lon")
    n_z = n_lon // 2
    width = wq.shape[0]
    lat, lon = lax.axis_index("lat"), lax.axis_index("lon")
    z, y_hi = lon // 2, lon % 2
    core = lat % 2
    sign = 1 - 2 * core

    def at(step, line):
        return lax.rem(z + step + n_z, n_z) * 2 + (y_hi if line == 0 else 1 - y_hi)

    partner = at(0, 1)
    sb, pk = (sb0, sb1), (pk0, pk1)
    lat_chip = lat + sign
    lat_off = lax.rem(lat + n_lat - sign, n_lat)
    lon_left, lon_right = lax.rem(lon + n_lon - 1, n_lon), lax.rem(lon + 1, n_lon)
    off_inside = jnp.where(core == 0, lat > 0, lat < n_lat - 1)

    loads = [
        pltpu.make_async_copy(tok, g.at[lon], load_sem.at[0]),
        pltpu.make_async_copy(wqkv, wq, load_sem.at[1]),
    ]
    for load in loads:
        load.start()

    sends = []

    def send(src, dst, sem, dev):
        if comm:
            copy = pltpu.make_async_remote_copy(
                src_ref=src,
                dst_ref=dst,
                send_sem=send_sem.at[len(sends)],
                recv_sem=sem,
                device_id=dev,
                device_id_type=MESH,
            )
            copy.start()
            sends.append(copy)

    def arrived(ref, sem):
        if comm:
            pltpu.make_async_remote_copy(
                src_ref=ref,
                dst_ref=ref,
                send_sem=send_sem.at[0],
                recv_sem=sem,
                device_id=(lat, partner),
                device_id_type=MESH,
            ).wait_recv()

    def send_g(owner, col, dev):
        send(g.at[owner, col], g.at[owner, col], g_sem.at[owner, col], dev)

    def wait_g(owner, col):
        arrived(g.at[owner, col], g_sem.at[owner, col])

    if comm:
        barrier = pltpu.get_barrier_semaphore()
        friends = [
            (lat, at(1, 0)),
            (lat, at(-1, 0)),
            (lat, partner),
            (lat_chip, lon),
            (lat_off, lon),
            (lat_off, lon_left),
            (lat_off, lon_right),
        ]
        for friend in friends:
            pl.semaphore_signal(barrier, inc=1, device_id=friend, device_id_type=MESH)
        pl.semaphore_wait(barrier, len(friends))

    up, down = (lat, at(1, 0)), (lat, at(-1, 0))
    across = (lat, partner)

    def send_own(col, dev):
        send(tok.at[col], g.at[lon, col], g_sem.at[lon, col], dev)

    send(ids_hbm, ids_in, ids_sem.at[0], across)
    send_own(0, across)
    send_own(1, across)
    send_own(1, up)
    send_own(1, down)
    send_own(0, up)
    send_own(0, down)
    send(tok, nb.at[pl.ds(0, 2)], n_sem.at[0], (lat_off, lon))
    send(tok.at[1], nb.at[2], n_sem.at[1], (lat_off, lon_right))
    send(tok.at[0], nb.at[3], n_sem.at[2], (lat_off, lon_left))

    def lookup(owner, table):
        col = jnp.int32(0)
        which = jnp.int32(0)
        for entry in range(2 * TELE):
            value = table[0, entry // TELE, entry % TELE]
            hit = lax.shift_right_logical(value, 1) == owner
            col = jnp.where(hit, value & 1, col)
            which = jnp.where(hit, jnp.int32(entry // TELE), which)
        return col, which

    def project(source, k_dst, v_dst):
        @pl.loop(0, width // 256, unroll=UNROLL)
        def _(step):
            cols = pl.ds(pl.multiple_of(step * 256, 256), 256)
            k_cols = pl.ds(pl.multiple_of(width + step * 256, 256), 256)
            k_dst[:, cols] = nn_dot(source[...], wq[:, k_cols]).astype(BF)
            v_dst[cols, :] = nt_dot(wvt[cols, :], source[...]).astype(BF)

    def pair_cols(pair):
        return pl.ds(pl.multiple_of(pair * 128, 128), 128)

    def pipelined(score, finish_pair):
        score(0, 0)

        @pl.loop(0, PAIRS // 2)
        def _(step):
            score(2 * step + 1, 1)
            finish_pair(2 * step, 0)
            score(jnp.minimum(2 * step + 2, PAIRS - 1), 0)
            finish_pair(2 * step + 1, 1)

    def near(keys_of, first):
        sizes = [size for _, _, size in keys_of(0)]
        count = sum(sizes)

        def score(pair, slot):
            cols = pair_cols(pair)
            for j in range(2):
                queries = qmt[j, pair]
                offset = j * count
                peak = None
                for row, start, size in keys_of(j):
                    s = nn_dot(kn[row, pl.ds(start, size), cols], queries)
                    sb[slot][pl.ds(offset, size)] = s
                    top = jnp.max(s, axis=0, keepdims=True)
                    peak = top if peak is None else jnp.maximum(peak, top)
                    offset += size
                pk[slot][j] = peak

        def finish_pair(pair, slot):
            cols = pair_cols(pair)
            for j in range(2):
                peak = pk[slot][j]
                if not first:
                    before = ms[j, pair]
                    peak = jnp.maximum(peak, before)
                total = None
                summed = None
                offset = j * count
                for row, start, size in keys_of(j):
                    expos = jnp.exp(sb[slot][pl.ds(offset, size)] - peak)
                    part = jnp.sum(expos, axis=0, keepdims=True)
                    prod = nn_dot(vn[row, cols, pl.ds(start, size)], expos.astype(BF))
                    total = part if total is None else total + part
                    summed = prod if summed is None else summed + prod
                    offset += size
                even, odd = summed[:HD, :BLOCK], summed[HD:, BLOCK:]
                if not first:
                    decay = jnp.exp(before - peak)
                    total = total + ls[j, pair] * decay
                    even = even + acc[j, pair, 0] * decay[:, :BLOCK]
                    odd = odd + acc[j, pair, 1] * decay[:, BLOCK:]
                ms[j, pair] = peak
                ls[j, pair] = total
                acc[j, pair, 0] = even
                acc[j, pair, 1] = odd

        pipelined(score, finish_pair)

    def far(tiles, own=False):
        whiches = []
        for i, (owner, both, one) in enumerate(tiles):
            col, which = lookup(owner, ids)
            whiches.append(which)
            rows = slice(i * BLOCK, (i + 1) * BLOCK)
            x[rows] = one[...] if both is None else jnp.where(col == 1, both[1], both[0])
        rows = pl.ds(0, len(tiles) * BLOCK)
        project(x.at[rows], kt.at[rows], vt.at[:, rows])
        if own:
            col, which = lookup(lon, ids)
            last = slice(len(tiles) * BLOCK, (len(tiles) + 1) * BLOCK)
            whiches.append(which)
            kt[last] = jnp.where(col == 1, kn[0, BLOCK : 2 * BLOCK], kn[0, :BLOCK])
            vt[:, last] = jnp.where(col == 1, vn[0, :, BLOCK : 2 * BLOCK], vn[0, :, :BLOCK])
        count = len(whiches)
        keys = count * BLOCK

        def score(pair, slot):
            cols = pair_cols(pair)
            for i in range(count):
                s = nn_dot(kt[i * BLOCK : (i + 1) * BLOCK, cols], qmt[whiches[i], pair])
                sb[slot][i * BLOCK : (i + 1) * BLOCK] = s
                pk[slot][i] = jnp.max(s, axis=0, keepdims=True)

        def finish_pair(pair, slot):
            cols = pair_cols(pair)
            peaks = [pk[slot][i] for i in range(count)]
            before = [ms[j, pair] for j in range(2)]
            now = []
            for j in range(2):
                peak = before[j]
                for i in range(count):
                    peak = jnp.maximum(peak, jnp.where(whiches[i] == j, peaks[i], before[j]))
                now.append(peak)
            decay = [jnp.exp(before[j] - now[j]) for j in range(2)]
            totals = [ls[j, pair] * decay[j] for j in range(2)]
            weights = [[], []]
            for i in range(count):
                mine = whiches[i] == 0
                expos = jnp.exp(sb[slot][i * BLOCK : (i + 1) * BLOCK] - jnp.where(mine, now[0], now[1]))
                part = jnp.sum(expos, axis=0, keepdims=True)
                rounded = expos.astype(BF)
                none = jnp.zeros_like(rounded)
                totals[0] = totals[0] + jnp.where(mine, part, 0.0)
                totals[1] = totals[1] + jnp.where(mine, 0.0, part)
                weights[0].append(jnp.where(mine, rounded, none))
                weights[1].append(jnp.where(mine, none, rounded))
            for j in range(2):
                summed = nn_dot(vt[cols, :keys], jnp.concatenate(weights[j], axis=0))
                ms[j, pair] = now[j]
                ls[j, pair] = totals[j]
                acc[j, pair, 0] = acc[j, pair, 0] * decay[j][:, :BLOCK] + summed[:HD, :BLOCK]
                acc[j, pair, 1] = acc[j, pair, 1] * decay[j][:, BLOCK:] + summed[HD:, BLOCK:]

        pipelined(score, finish_pair)

    def own_projection():
        own = g.at[lon]

        @pl.loop(0, width // 128)
        def _(step):
            cols = pl.ds(pl.multiple_of(step * 128, 128), 128)
            v_cols = pl.ds(pl.multiple_of(2 * width + step * 128, 128), 128)
            wvt[cols, :] = wq[:, v_cols].T

        @pl.loop(0, width // 256)
        def _(step):
            cols = pl.ds(pl.multiple_of(step * 256, 256), 256)
            tokens = own[...].reshape(2 * BLOCK, width)
            queries = nn_dot(tokens, wq[:, cols]).astype(BF).astype(F32) * HD**-0.5
            row = lax.broadcasted_iota(jnp.int32, (BLOCK, BLOCK), 0)
            for j in range(2):
                for half in range(2):
                    block = queries[j * BLOCK : (j + 1) * BLOCK, half * 128 : (half + 1) * 128].T
                    even = jnp.where(row < HD, block, 0.0)
                    odd = jnp.where(row < HD, 0.0, block)
                    qmt[j, step * 2 + half] = jnp.concatenate([even, odd], axis=1).astype(BF)
        x[: 2 * BLOCK] = own[...].reshape(2 * BLOCK, width)
        project(x.at[pl.ds(0, 256)], kn.at[0, pl.ds(0, 256)], vn.at[0, :, pl.ds(0, 256)])

    def finish():
        @pl.loop(0, PAIRS)
        def _(pair):
            cols = pair_cols(pair)
            for j in range(2):
                total = ls[j, pair]
                even = acc[j, pair, 0] / total[:, :BLOCK]
                odd = acc[j, pair, 1] / total[:, BLOCK:]
                out[j * BLOCK : (j + 1) * BLOCK, cols] = jnp.concatenate([even, odd], axis=0).T.astype(BF)

    def onward(owner, col, direction):
        send_g(owner, col, up if direction > 0 else down)

    def relay(step, col):
        wait_g(at(-step, 0), col)
        wait_g(at(step, 0), col)
        onward(at(-step, 0), col, 1)
        onward(at(step, 0), col, -1)

    def select(slot, owner):
        if comm:
            col, _ = lookup(owner, ids_across)
            pick[slot] = jnp.where(col == 1, g[owner, 1], g[owner, 0])

    def hand(slot):
        send(pick.at[slot], picked.at[slot], pick_sem.at[slot], across)

    def given(slot):
        arrived(picked.at[slot], pick_sem.at[slot])

    def both(step, line):
        owner = at(step, line)
        return owner, g.at[owner], None

    def single(step, slot):
        return at(step, 1), None, picked.at[slot]

    for load in loads:
        load.wait()
    if compute:
        own_projection()

    chip = (lat_chip, lon)
    send(kn.at[0, pl.ds(0, 256)], kn.at[1, pl.ds(0, 256)], chip_sem.at[0], chip)
    send(vn.at[0, :, pl.ds(0, 256)], vn.at[1, :, pl.ds(0, 256)], chip_sem.at[1], chip)
    relay(1, 1)
    if comm:
        arrived(ids_in, ids_sem.at[0])
        table = pltpu.make_async_copy(ids_in, ids_across, ids_sem.at[1])
        table.start()
        table.wait()
    arrived(kn.at[1, pl.ds(0, 256)], chip_sem.at[0])
    arrived(vn.at[1, :, pl.ds(0, 256)], chip_sem.at[1])
    if compute:
        near(lambda j: ((0, 0, 256), (1, 0, 256)), True)
    relay(1, 0)

    wait_g(partner, 0)
    wait_g(partner, 1)
    if compute:
        far([both(0, 1), both(-1, 0), both(1, 0)], own=True)

    relay(2, 1)
    relay(2, 0)
    turn = 1 - 2 * y_hi
    ahead = (lat, lax.rem(z + turn + n_z, n_z) * 2 + y_hi)
    behind = (lat, lax.rem(z - turn + n_z, n_z) * 2 + y_hi)
    send_g(partner, 1 - y_hi, ahead)
    select(0, at(-2, 0))
    select(1, at(2, 0))
    hand(0)
    hand(1)

    arrived(nb.at[pl.ds(0, 2)], n_sem.at[0])
    arrived(nb.at[2], n_sem.at[1])
    arrived(nb.at[3], n_sem.at[2])
    if compute:
        @pl.when(off_inside)
        def _():
            project(nb.reshape(4 * BLOCK, width), kn.at[2], vn.at[2])
            near(lambda j: ((2, 0, 256), (2, 256 + j * BLOCK, BLOCK)), False)

    last = lax.rem(z + n_z - 3 * sign, n_z) * 2 + y_hi
    beyond = (lat, lax.rem(z + n_z + sign, n_z) * 2 + y_hi)
    wait_g(at(-3, 0), 1)
    wait_g(at(3, 0), 1)
    send_g(last, 1, beyond)
    if compute:
        far([both(-2, 0), both(2, 0)])
    wait_g(at(-3, 0), 0)
    wait_g(at(3, 0), 0)
    send_g(last, 0, beyond)
    select(2, at(-3, 0))
    select(3, at(3, 0))
    send_g(partner, 1 - y_hi, behind)
    send_g(partner, y_hi, ahead)
    send_g(partner, y_hi, behind)
    hand(2)
    hand(3)
    if compute:
        far([both(-3, 0), both(3, 0)])

    wait_g(lax.rem(z - turn + n_z, n_z) * 2 + 1 - y_hi, 1 - y_hi)
    if compute:
        x[0:128] = g[lon_left, 1]
        x[128:256] = g[lon_right, 0]
        project(x.at[pl.ds(0, 256)], kn.at[0, pl.ds(256, 256)], vn.at[0, :, pl.ds(256, 256)])
    wait_g(at(4, 0), 1)
    wait_g(at(4, 0), 0)
    select(4, at(4, 0))
    send(kn.at[0, pl.ds(256, 256)], kn.at[1, pl.ds(256, 256)], chip_sem.at[2], chip)
    send(vn.at[0, :, pl.ds(256, 256)], vn.at[1, :, pl.ds(256, 256)], chip_sem.at[3], chip)
    hand(4)

    given(0)
    given(1)
    if compute:
        far([single(-2, 0), single(2, 1), both(4, 0)])
    arrived(kn.at[1, pl.ds(256, 256)], chip_sem.at[2])
    arrived(vn.at[1, :, pl.ds(256, 256)], chip_sem.at[3])
    if compute:
        near(lambda j: ((0, 256 + j * BLOCK, BLOCK), (1, 256 + j * BLOCK, BLOCK)), False)

    wait_g(lax.rem(z + turn + n_z, n_z) * 2 + 1 - y_hi, 1 - y_hi)
    wait_g(at(-1, 1), y_hi)
    wait_g(at(1, 1), y_hi)
    if compute:
        far([both(-1, 1), both(1, 1)])
    given(2)
    given(3)
    if compute:
        far([single(-3, 2), single(3, 3)])
    given(4)
    if compute:
        far([single(4, 4)])
        finish()
    else:
        out[...] = g[lon].reshape(out.shape)
    for copy in sends:
        copy.wait_send()


def on_device(tokens, w_qkv, w_out, tele_ids, comm=True, compute=True):
    shape = tokens.shape
    width = shape[3]
    tokens = tokens.reshape(2, BLOCK, width)
    n_lon = lax.axis_size("lon")
    anywhere = pl.BlockSpec(memory_space=pl.ANY)
    attended = pl.pallas_call(
        functools.partial(layer_kernel, comm, compute),
        out_shape=jax.ShapeDtypeStruct((2 * BLOCK, width), BF),
        in_specs=[pl.BlockSpec(memory_space=pltpu.SMEM)] + [anywhere] * 3,
        out_specs=pl.BlockSpec(memory_space=pltpu.VMEM),
        scratch_shapes=[
            pltpu.VMEM((n_lon, 2, BLOCK, width), BF),
            pltpu.VMEM((4, BLOCK, width), BF),
            pltpu.VMEM((5, BLOCK, width), BF),
            pltpu.VMEM((5, BLOCK, width), BF),
            pltpu.VMEM((width, 3 * width), BF),
            pltpu.VMEM((width, width), BF),
            pltpu.VMEM((4 * BLOCK, width), BF),
            pltpu.VMEM((3, 4 * BLOCK, width), BF),
            pltpu.VMEM((3, width, 4 * BLOCK), BF),
            pltpu.VMEM((4 * BLOCK, width), BF),
            pltpu.VMEM((width, 4 * BLOCK), BF),
            pltpu.VMEM((2, PAIRS, 2 * HD, 2 * BLOCK), BF),
            pltpu.VMEM((2, PAIRS, 1, 2 * BLOCK), F32),
            pltpu.VMEM((2, PAIRS, 1, 2 * BLOCK), F32),
            pltpu.VMEM((2, PAIRS, 2, HD, BLOCK), F32),
            pltpu.VMEM((8 * BLOCK, 2 * BLOCK), F32),
            pltpu.VMEM((8 * BLOCK, 2 * BLOCK), F32),
            pltpu.VMEM((4, 1, 2 * BLOCK), F32),
            pltpu.VMEM((4, 1, 2 * BLOCK), F32),
            pltpu.VMEM((1, 2, TELE), jnp.int32),
            pltpu.SMEM((1, 2, TELE), jnp.int32),
            pltpu.SemaphoreType.DMA((SENDS,)),
            pltpu.SemaphoreType.DMA((n_lon, 2)),
            pltpu.SemaphoreType.DMA((3,)),
            pltpu.SemaphoreType.DMA((4,)),
            pltpu.SemaphoreType.DMA((5,)),
            pltpu.SemaphoreType.DMA((2,)),
            pltpu.SemaphoreType.DMA((2,)),
        ],
        compiler_params=pltpu.CompilerParams(
            collective_id=0 if comm else None, has_side_effects=True, vmem_limit_bytes=60 * 1024 * 1024
        ),
        name="layer",
    )(tele_ids, tele_ids, tokens, w_qkv)
    mixed = jnp.dot(attended, w_out, preferred_element_type=F32).astype(BF)
    return mixed.reshape(shape)


def solution(mesh):
    return jax.shard_map(
        on_device,
        mesh=mesh,
        in_specs=(P("lat", "lon", None, None), P(), P(), P("lat", "lon", None)),
        out_specs=P("lat", "lon", None, None),
        check_vma=False,
    )
```

```python
import functools

import jax
import jax.numpy as jnp
from jax import lax
from jax.experimental import pallas as pl
from jax.experimental.pallas import tpu as pltpu
from jax.sharding import PartitionSpec as P

MESH = pl.DeviceIdType.MESH
BF = jnp.bfloat16
F32 = jnp.float32
H = 16
HD = 64
BLOCK = 128
PAIRS = H // 2
SENDS = 40
TELE = 8
UNROLL = 2
SPAN = 4


def nt_dot(a, b):
    return lax.dot_general(a, b, (((1,), (1,)), ((), ())), preferred_element_type=F32)


def nn_dot(a, b):
    return jnp.dot(a, b, preferred_element_type=F32)


def layer_kernel(
    comm,
    compute,
    ids,
    ids_hbm,
    tok,
    wqkv,
    out,
    g,
    nb,
    pick,
    picked,
    wq,
    wvt,
    x,
    kn,
    vn,
    kt,
    vt,
    qmt,
    ms,
    ls,
    acc,
    sb0,
    sb1,
    pk0,
    pk1,
    ids_in,
    ids_across,
    send_sem,
    g_sem,
    n_sem,
    chip_sem,
    pick_sem,
    ids_sem,
    load_sem,
):
    n_lat, n_lon = lax.axis_size("lat"), lax.axis_size("lon")
    n_z = n_lon // 2
    width = wq.shape[0]
    lat, lon = lax.axis_index("lat"), lax.axis_index("lon")
    z, y_hi = lon // 2, lon % 2
    core = lat % 2
    sign = 1 - 2 * core

    def at(step, line):
        return lax.rem(z + step + n_z, n_z) * 2 + (y_hi if line == 0 else 1 - y_hi)

    partner = at(0, 1)
    sb, pk = (sb0, sb1), (pk0, pk1)
    lat_chip = lat + sign
    lat_off = lax.rem(lat + n_lat - sign, n_lat)
    lon_left, lon_right = lax.rem(lon + n_lon - 1, n_lon), lax.rem(lon + 1, n_lon)
    off_inside = jnp.where(core == 0, lat > 0, lat < n_lat - 1)

    loads = [
        pltpu.make_async_copy(tok, g.at[lon], load_sem.at[0]),
        pltpu.make_async_copy(wqkv, wq, load_sem.at[1]),
    ]
    for load in loads:
        load.start()

    sends = []

    def send(src, dst, sem, dev):
        if comm:
            copy = pltpu.make_async_remote_copy(
                src_ref=src,
                dst_ref=dst,
                send_sem=send_sem.at[len(sends)],
                recv_sem=sem,
                device_id=dev,
                device_id_type=MESH,
            )
            copy.start()
            sends.append(copy)

    def arrived(ref, sem):
        if comm:
            pltpu.make_async_remote_copy(
                src_ref=ref,
                dst_ref=ref,
                send_sem=send_sem.at[0],
                recv_sem=sem,
                device_id=(lat, partner),
                device_id_type=MESH,
            ).wait_recv()

    def send_g(owner, col, dev):
        send(g.at[owner, col], g.at[owner, col], g_sem.at[owner, col], dev)

    def wait_g(owner, col):
        arrived(g.at[owner, col], g_sem.at[owner, col])

    if comm:
        barrier = pltpu.get_barrier_semaphore()
        friends = [
            (lat, at(1, 0)),
            (lat, at(-1, 0)),
            (lat, partner),
            (lat_chip, lon),
            (lat_off, lon),
            (lat_off, lon_left),
            (lat_off, lon_right),
        ]
        for friend in friends:
            pl.semaphore_signal(barrier, inc=1, device_id=friend, device_id_type=MESH)
        pl.semaphore_wait(barrier, len(friends))

    up, down = (lat, at(1, 0)), (lat, at(-1, 0))
    across = (lat, partner)

    def send_own(col, dev):
        send(tok.at[col], g.at[lon, col], g_sem.at[lon, col], dev)

    send(ids_hbm, ids_in, ids_sem.at[0], across)
    send(tok, nb.at[pl.ds(0, 2)], n_sem.at[0], (lat_off, lon))
    send(tok.at[1], nb.at[2], n_sem.at[1], (lat_off, lon_right))
    send(tok.at[0], nb.at[3], n_sem.at[2], (lat_off, lon_left))
    send_own(1, up)
    send_own(1, down)
    send_own(0, up)
    send_own(0, down)
    send_own(0, across)
    send_own(1, across)

    def lookup(owner, table):
        col = jnp.int32(0)
        which = jnp.int32(0)
        for entry in range(2 * TELE):
            value = table[0, entry // TELE, entry % TELE]
            hit = lax.shift_right_logical(value, 1) == owner
            col = jnp.where(hit, value & 1, col)
            which = jnp.where(hit, jnp.int32(entry // TELE), which)
        return col, which

    def project(source, k_dst, v_dst):
        @pl.loop(0, width // 256, unroll=UNROLL)
        def _(step):
            cols = pl.ds(pl.multiple_of(step * 256, 256), 256)
            k_cols = pl.ds(pl.multiple_of(width + step * 256, 256), 256)
            k_dst[:, cols] = nn_dot(source[...], wq[:, k_cols]).astype(BF)
            v_dst[cols, :] = nt_dot(wvt[cols, :], source[...]).astype(BF)

    def pair_cols(pair):
        return pl.ds(pl.multiple_of(pair * 128, 128), 128)

    def pipelined(score, finish_pair):
        score(0, 0)

        @pl.loop(0, PAIRS // SPAN)
        def _(step):
            for k in range(SPAN):
                pair = step * SPAN + k
                score(jnp.minimum(pair + 1, PAIRS - 1), (k + 1) % 2)
                finish_pair(pair, k % 2)

    def near(keys_of, first):
        sizes = [size for _, _, size in keys_of(0)]
        count = sum(sizes)

        def score(pair, slot):
            cols = pair_cols(pair)
            for j in range(2):
                queries = qmt[j, pair]
                offset = j * count
                peak = None
                for row, start, size in keys_of(j):
                    s = nn_dot(kn[row, pl.ds(start, size), cols], queries)
                    sb[slot][pl.ds(offset, size)] = s
                    top = jnp.max(s, axis=0, keepdims=True)
                    peak = top if peak is None else jnp.maximum(peak, top)
                    offset += size
                pk[slot][j] = peak

        def finish_pair(pair, slot):
            cols = pair_cols(pair)
            for j in range(2):
                peak = pk[slot][j]
                if not first:
                    before = ms[j, pair]
                    peak = jnp.maximum(peak, before)
                total = None
                summed = None
                offset = j * count
                for row, start, size in keys_of(j):
                    expos = jnp.exp(sb[slot][pl.ds(offset, size)] - peak)
                    part = jnp.sum(expos, axis=0, keepdims=True)
                    prod = nn_dot(vn[row, cols, pl.ds(start, size)], expos.astype(BF))
                    total = part if total is None else total + part
                    summed = prod if summed is None else summed + prod
                    offset += size
                even, odd = summed[:HD, :BLOCK], summed[HD:, BLOCK:]
                if not first:
                    decay = jnp.exp(before - peak)
                    total = total + ls[j, pair] * decay
                    even = even + acc[j, pair, 0] * decay[:, :BLOCK]
                    odd = odd + acc[j, pair, 1] * decay[:, BLOCK:]
                ms[j, pair] = peak
                ls[j, pair] = total
                acc[j, pair, 0] = even
                acc[j, pair, 1] = odd

        pipelined(score, finish_pair)

    def far(tiles, own=False):
        whiches = []
        for i, (owner, both, one) in enumerate(tiles):
            col, which = lookup(owner, ids)
            whiches.append(which)
            rows = slice(i * BLOCK, (i + 1) * BLOCK)
            x[rows] = one[...] if both is None else jnp.where(col == 1, both[1], both[0])
        rows = pl.ds(0, len(tiles) * BLOCK)
        project(x.at[rows], kt.at[rows], vt.at[:, rows])
        if own:
            col, which = lookup(lon, ids)
            last = slice(len(tiles) * BLOCK, (len(tiles) + 1) * BLOCK)
            whiches.append(which)
            kt[last] = jnp.where(col == 1, kn[0, BLOCK : 2 * BLOCK], kn[0, :BLOCK])
            vt[:, last] = jnp.where(col == 1, vn[0, :, BLOCK : 2 * BLOCK], vn[0, :, :BLOCK])
        count = len(whiches)
        keys = count * BLOCK

        def score(pair, slot):
            cols = pair_cols(pair)
            for i in range(count):
                s = nn_dot(kt[i * BLOCK : (i + 1) * BLOCK, cols], qmt[whiches[i], pair])
                sb[slot][i * BLOCK : (i + 1) * BLOCK] = s
                pk[slot][i] = jnp.max(s, axis=0, keepdims=True)

        def finish_pair(pair, slot):
            cols = pair_cols(pair)
            peaks = [pk[slot][i] for i in range(count)]
            before = [ms[j, pair] for j in range(2)]
            now = []
            for j in range(2):
                peak = before[j]
                for i in range(count):
                    peak = jnp.maximum(peak, jnp.where(whiches[i] == j, peaks[i], before[j]))
                now.append(peak)
            decay = [jnp.exp(before[j] - now[j]) for j in range(2)]
            totals = [ls[j, pair] * decay[j] for j in range(2)]
            weights = [[], []]
            for i in range(count):
                mine = whiches[i] == 0
                expos = jnp.exp(sb[slot][i * BLOCK : (i + 1) * BLOCK] - jnp.where(mine, now[0], now[1]))
                part = jnp.sum(expos, axis=0, keepdims=True)
                rounded = expos.astype(BF)
                none = jnp.zeros_like(rounded)
                totals[0] = totals[0] + jnp.where(mine, part, 0.0)
                totals[1] = totals[1] + jnp.where(mine, 0.0, part)
                weights[0].append(jnp.where(mine, rounded, none))
                weights[1].append(jnp.where(mine, none, rounded))
            for j in range(2):
                summed = nn_dot(vt[cols, :keys], jnp.concatenate(weights[j], axis=0))
                ms[j, pair] = now[j]
                ls[j, pair] = totals[j]
                acc[j, pair, 0] = acc[j, pair, 0] * decay[j][:, :BLOCK] + summed[:HD, :BLOCK]
                acc[j, pair, 1] = acc[j, pair, 1] * decay[j][:, BLOCK:] + summed[HD:, BLOCK:]

        pipelined(score, finish_pair)

    def own_projection():
        own = g.at[lon]

        @pl.loop(0, width // 128)
        def _(step):
            cols = pl.ds(pl.multiple_of(step * 128, 128), 128)
            v_cols = pl.ds(pl.multiple_of(2 * width + step * 128, 128), 128)
            wvt[cols, :] = wq[:, v_cols].T

        @pl.loop(0, width // 256)
        def _(step):
            cols = pl.ds(pl.multiple_of(step * 256, 256), 256)
            tokens = own[...].reshape(2 * BLOCK, width)
            queries = nn_dot(tokens, wq[:, cols]).astype(BF).astype(F32) * HD**-0.5
            row = lax.broadcasted_iota(jnp.int32, (BLOCK, BLOCK), 0)
            for j in range(2):
                for half in range(2):
                    block = queries[j * BLOCK : (j + 1) * BLOCK, half * 128 : (half + 1) * 128].T
                    even = jnp.where(row < HD, block, 0.0)
                    odd = jnp.where(row < HD, 0.0, block)
                    qmt[j, step * 2 + half] = jnp.concatenate([even, odd], axis=1).astype(BF)
        x[: 2 * BLOCK] = own[...].reshape(2 * BLOCK, width)
        project(x.at[pl.ds(0, 256)], kn.at[0, pl.ds(0, 256)], vn.at[0, :, pl.ds(0, 256)])

    def finish():
        @pl.loop(0, PAIRS)
        def _(pair):
            cols = pair_cols(pair)
            for j in range(2):
                total = ls[j, pair]
                even = acc[j, pair, 0] / total[:, :BLOCK]
                odd = acc[j, pair, 1] / total[:, BLOCK:]
                out[j * BLOCK : (j + 1) * BLOCK, cols] = jnp.concatenate([even, odd], axis=0).T.astype(BF)

    def onward(owner, col, direction):
        send_g(owner, col, up if direction > 0 else down)

    def relay(step, col):
        wait_g(at(-step, 0), col)
        wait_g(at(step, 0), col)
        onward(at(-step, 0), col, 1)
        onward(at(step, 0), col, -1)

    def select(slot, owner):
        if comm:
            col, _ = lookup(owner, ids_across)
            pick[slot] = jnp.where(col == 1, g[owner, 1], g[owner, 0])

    def hand(slot):
        send(pick.at[slot], picked.at[slot], pick_sem.at[slot], across)

    def given(slot):
        arrived(picked.at[slot], pick_sem.at[slot])

    def both(step, line):
        owner = at(step, line)
        return owner, g.at[owner], None

    def single(step, slot):
        return at(step, 1), None, picked.at[slot]

    for load in loads:
        load.wait()
    if compute:
        own_projection()

    chip = (lat_chip, lon)
    send(kn.at[0, pl.ds(0, 256)], kn.at[1, pl.ds(0, 256)], chip_sem.at[0], chip)
    send(vn.at[0, :, pl.ds(0, 256)], vn.at[1, :, pl.ds(0, 256)], chip_sem.at[1], chip)
    relay(1, 1)
    if comm:
        arrived(ids_in, ids_sem.at[0])
        table = pltpu.make_async_copy(ids_in, ids_across, ids_sem.at[1])
        table.start()
        table.wait()
    arrived(kn.at[1, pl.ds(0, 256)], chip_sem.at[0])
    arrived(vn.at[1, :, pl.ds(0, 256)], chip_sem.at[1])
    if compute:
        near(lambda j: ((0, 0, 256), (1, 0, 256)), True)
    relay(1, 0)

    arrived(nb.at[pl.ds(0, 2)], n_sem.at[0])
    arrived(nb.at[2], n_sem.at[1])
    arrived(nb.at[3], n_sem.at[2])
    if compute:
        @pl.when(off_inside)
        def _():
            project(nb.reshape(4 * BLOCK, width), kn.at[2], vn.at[2])
            near(lambda j: ((2, 0, 256), (2, 256 + j * BLOCK, BLOCK)), False)

    relay(2, 1)
    relay(2, 0)
    select(0, at(-2, 0))
    select(1, at(2, 0))
    hand(0)
    hand(1)
    if compute:
        far([both(-1, 0), both(1, 0)], own=True)

    wait_g(partner, 0)
    wait_g(partner, 1)
    turn = 1 - 2 * y_hi
    ahead = (lat, lax.rem(z + turn + n_z, n_z) * 2 + y_hi)
    behind = (lat, lax.rem(z - turn + n_z, n_z) * 2 + y_hi)
    send_g(partner, 1 - y_hi, ahead)
    if compute:
        far([both(0, 1), both(-2, 0), both(2, 0)])

    last = lax.rem(z + n_z - 3 * sign, n_z) * 2 + y_hi
    beyond = (lat, lax.rem(z + n_z + sign, n_z) * 2 + y_hi)
    wait_g(at(-3, 0), 1)
    wait_g(at(3, 0), 1)
    send_g(last, 1, beyond)
    wait_g(at(-3, 0), 0)
    wait_g(at(3, 0), 0)
    send_g(last, 0, beyond)
    select(2, at(-3, 0))
    select(3, at(3, 0))
    send_g(partner, 1 - y_hi, behind)
    send_g(partner, y_hi, ahead)
    send_g(partner, y_hi, behind)
    hand(2)
    hand(3)

    given(0)
    given(1)
    if compute:
        far([both(-3, 0), both(3, 0), single(-2, 0), single(2, 1)])
    wait_g(at(4, 0), 1)
    wait_g(at(4, 0), 0)
    select(4, at(4, 0))
    wait_g(lax.rem(z - turn + n_z, n_z) * 2 + 1 - y_hi, 1 - y_hi)
    hand(4)
    if compute:
        x[0:128] = g[lon_left, 1]
        x[128:256] = g[lon_right, 0]
        project(x.at[pl.ds(0, 256)], kn.at[0, pl.ds(256, 256)], vn.at[0, :, pl.ds(256, 256)])
    wait_g(lax.rem(z + turn + n_z, n_z) * 2 + 1 - y_hi, 1 - y_hi)
    send(kn.at[0, pl.ds(256, 256)], kn.at[1, pl.ds(256, 256)], chip_sem.at[2], chip)
    send(vn.at[0, :, pl.ds(256, 256)], vn.at[1, :, pl.ds(256, 256)], chip_sem.at[3], chip)
    wait_g(at(-1, 1), y_hi)
    wait_g(at(1, 1), y_hi)
    if compute:
        far([both(-1, 1), both(1, 1), both(4, 0)])
    arrived(kn.at[1, pl.ds(256, 256)], chip_sem.at[2])
    arrived(vn.at[1, :, pl.ds(256, 256)], chip_sem.at[3])
    if compute:
        near(lambda j: ((0, 256 + j * BLOCK, BLOCK), (1, 256 + j * BLOCK, BLOCK)), False)
    given(2)
    given(3)
    given(4)
    if compute:
        far([single(-3, 2), single(3, 3), single(4, 4)])
        finish()
    else:
        out[...] = g[lon].reshape(out.shape)
    for copy in sends:
        copy.wait_send()


def on_device(tokens, w_qkv, w_out, tele_ids, comm=True, compute=True):
    shape = tokens.shape
    width = shape[3]
    tokens = tokens.reshape(2, BLOCK, width)
    n_lon = lax.axis_size("lon")
    anywhere = pl.BlockSpec(memory_space=pl.ANY)
    attended = pl.pallas_call(
        functools.partial(layer_kernel, comm, compute),
        out_shape=jax.ShapeDtypeStruct((2 * BLOCK, width), BF),
        in_specs=[pl.BlockSpec(memory_space=pltpu.SMEM)] + [anywhere] * 3,
        out_specs=pl.BlockSpec(memory_space=pltpu.VMEM),
        scratch_shapes=[
            pltpu.VMEM((n_lon, 2, BLOCK, width), BF),
            pltpu.VMEM((4, BLOCK, width), BF),
            pltpu.VMEM((5, BLOCK, width), BF),
            pltpu.VMEM((5, BLOCK, width), BF),
            pltpu.VMEM((width, 3 * width), BF),
            pltpu.VMEM((width, width), BF),
            pltpu.VMEM((4 * BLOCK, width), BF),
            pltpu.VMEM((3, 4 * BLOCK, width), BF),
            pltpu.VMEM((3, width, 4 * BLOCK), BF),
            pltpu.VMEM((4 * BLOCK, width), BF),
            pltpu.VMEM((width, 4 * BLOCK), BF),
            pltpu.VMEM((2, PAIRS, 2 * HD, 2 * BLOCK), BF),
            pltpu.VMEM((2, PAIRS, 1, 2 * BLOCK), F32),
            pltpu.VMEM((2, PAIRS, 1, 2 * BLOCK), F32),
            pltpu.VMEM((2, PAIRS, 2, HD, BLOCK), F32),
            pltpu.VMEM((8 * BLOCK, 2 * BLOCK), F32),
            pltpu.VMEM((8 * BLOCK, 2 * BLOCK), F32),
            pltpu.VMEM((4, 1, 2 * BLOCK), F32),
            pltpu.VMEM((4, 1, 2 * BLOCK), F32),
            pltpu.VMEM((1, 2, TELE), jnp.int32),
            pltpu.SMEM((1, 2, TELE), jnp.int32),
            pltpu.SemaphoreType.DMA((SENDS,)),
            pltpu.SemaphoreType.DMA((n_lon, 2)),
            pltpu.SemaphoreType.DMA((3,)),
            pltpu.SemaphoreType.DMA((4,)),
            pltpu.SemaphoreType.DMA((5,)),
            pltpu.SemaphoreType.DMA((2,)),
            pltpu.SemaphoreType.DMA((2,)),
        ],
        compiler_params=pltpu.CompilerParams(
            collective_id=0 if comm else None, has_side_effects=True, vmem_limit_bytes=60 * 1024 * 1024
        ),
        name="layer",
    )(tele_ids, tele_ids, tokens, w_qkv)
    mixed = jnp.dot(attended, w_out, preferred_element_type=F32).astype(BF)
    return mixed.reshape(shape)


def solution(mesh):
    return jax.shard_map(
        on_device,
        mesh=mesh,
        in_specs=(P("lat", "lon", None, None), P(), P(), P("lat", "lon", None)),
        out_specs=P("lat", "lon", None, None),
        check_vma=False,
    )
```

```python
import functools

import jax
import jax.numpy as jnp
from jax import lax
from jax.experimental import pallas as pl
from jax.experimental.pallas import tpu as pltpu
from jax.sharding import PartitionSpec as P

MESH = pl.DeviceIdType.MESH
BF = jnp.bfloat16
F32 = jnp.float32
H = 16
HD = 64
BLOCK = 128
PAIRS = H // 2
SENDS = 40
TELE = 8
UNROLL = 2
SPAN = 4


def nt_dot(a, b):
    return lax.dot_general(a, b, (((1,), (1,)), ((), ())), preferred_element_type=F32)


def nn_dot(a, b):
    return jnp.dot(a, b, preferred_element_type=F32)


def layer_kernel(
    comm,
    compute,
    ids,
    ids_hbm,
    tok,
    wqkv,
    out,
    g,
    nb,
    pick,
    picked,
    wq,
    wvt,
    x,
    kn,
    vn,
    kt,
    vt,
    qmt,
    ms,
    ls,
    acc,
    sb0,
    sb1,
    pk0,
    pk1,
    ids_in,
    ids_peers,
    send_sem,
    g_sem,
    n_sem,
    chip_sem,
    pick_sem,
    ids_sem,
    load_sem,
):
    n_lat, n_lon = lax.axis_size("lat"), lax.axis_size("lon")
    n_z = n_lon // 2
    width = wq.shape[0]
    lat, lon = lax.axis_index("lat"), lax.axis_index("lon")
    z, y_hi = lon // 2, lon % 2
    core = lat % 2
    sign = 1 - 2 * core

    def at(step, line):
        return lax.rem(z + step + n_z, n_z) * 2 + (y_hi if line == 0 else 1 - y_hi)

    partner = at(0, 1)
    sb, pk = (sb0, sb1), (pk0, pk1)
    lat_chip = lat + sign
    lat_off = lax.rem(lat + n_lat - sign, n_lat)
    lon_left, lon_right = lax.rem(lon + n_lon - 1, n_lon), lax.rem(lon + 1, n_lon)
    off_inside = jnp.where(core == 0, lat > 0, lat < n_lat - 1)

    loads = [
        pltpu.make_async_copy(tok, g.at[lon], load_sem.at[0]),
        pltpu.make_async_copy(wqkv, wq, load_sem.at[1]),
    ]
    for load in loads:
        load.start()

    sends = []

    def send(src, dst, sem, dev):
        if comm:
            copy = pltpu.make_async_remote_copy(
                src_ref=src,
                dst_ref=dst,
                send_sem=send_sem.at[len(sends)],
                recv_sem=sem,
                device_id=dev,
                device_id_type=MESH,
            )
            copy.start()
            sends.append(copy)

    def arrived(ref, sem):
        if comm:
            pltpu.make_async_remote_copy(
                src_ref=ref,
                dst_ref=ref,
                send_sem=send_sem.at[0],
                recv_sem=sem,
                device_id=(lat, partner),
                device_id_type=MESH,
            ).wait_recv()

    def send_g(owner, col, dev):
        send(g.at[owner, col], g.at[owner, col], g_sem.at[owner, col], dev)

    def wait_g(owner, col):
        arrived(g.at[owner, col], g_sem.at[owner, col])

    if comm:
        barrier = pltpu.get_barrier_semaphore()
        friends = [
            (lat, at(1, 0)),
            (lat, at(-1, 0)),
            (lat, partner),
            (lat_chip, lon),
            (lat_off, lon),
            (lat_off, lon_left),
            (lat_off, lon_right),
        ]
        for friend in friends:
            pl.semaphore_signal(barrier, inc=1, device_id=friend, device_id_type=MESH)
        pl.semaphore_wait(barrier, len(friends))

    up, down = (lat, at(1, 0)), (lat, at(-1, 0))
    across = (lat, partner)

    def send_own(col, dev):
        send(tok.at[col], g.at[lon, col], g_sem.at[lon, col], dev)

    send(ids_hbm, ids_in.at[0], ids_sem.at[0], across)
    send(ids_hbm, ids_in.at[2], ids_sem.at[2], up)
    send(ids_hbm, ids_in.at[1], ids_sem.at[1], down)
    send(tok, nb.at[pl.ds(0, 2)], n_sem.at[0], (lat_off, lon))
    send(tok.at[1], nb.at[2], n_sem.at[1], (lat_off, lon_right))
    send(tok.at[0], nb.at[3], n_sem.at[2], (lat_off, lon_left))
    send_own(1, up)
    send_own(1, down)
    send_own(0, up)
    send_own(0, down)
    send_own(0, across)
    send_own(1, across)

    def lookup(owner, table, peer=None):
        col = jnp.int32(0)
        which = jnp.int32(0)
        for entry in range(2 * TELE):
            value = table[0, entry // TELE, entry % TELE] if peer is None else table[peer, 0, entry // TELE, entry % TELE]
            hit = lax.shift_right_logical(value, 1) == owner
            col = jnp.where(hit, value & 1, col)
            which = jnp.where(hit, jnp.int32(entry // TELE), which)
        return col, which

    def project(source, k_dst, v_dst):
        @pl.loop(0, width // 256, unroll=UNROLL)
        def _(step):
            cols = pl.ds(pl.multiple_of(step * 256, 256), 256)
            k_cols = pl.ds(pl.multiple_of(width + step * 256, 256), 256)
            k_dst[:, cols] = nn_dot(source[...], wq[:, k_cols]).astype(BF)
            v_dst[cols, :] = nt_dot(wvt[cols, :], source[...]).astype(BF)

    def pair_cols(pair):
        return pl.ds(pl.multiple_of(pair * 128, 128), 128)

    def pipelined(score, finish_pair):
        score(0, 0)

        @pl.loop(0, PAIRS // SPAN)
        def _(step):
            for k in range(SPAN):
                pair = step * SPAN + k
                score(jnp.minimum(pair + 1, PAIRS - 1), (k + 1) % 2)
                finish_pair(pair, k % 2)

    def near(keys_of, first):
        sizes = [size for _, _, size in keys_of(0)]
        count = sum(sizes)

        def score(pair, slot):
            cols = pair_cols(pair)
            for j in range(2):
                queries = qmt[j, pair]
                offset = j * count
                peak = None
                for row, start, size in keys_of(j):
                    s = nn_dot(kn[row, pl.ds(start, size), cols], queries)
                    sb[slot][pl.ds(offset, size)] = s
                    top = jnp.max(s, axis=0, keepdims=True)
                    peak = top if peak is None else jnp.maximum(peak, top)
                    offset += size
                pk[slot][j] = peak

        def finish_pair(pair, slot):
            cols = pair_cols(pair)
            for j in range(2):
                peak = pk[slot][j]
                if not first:
                    before = ms[j, pair]
                    peak = jnp.maximum(peak, before)
                total = None
                summed = None
                offset = j * count
                for row, start, size in keys_of(j):
                    expos = jnp.exp(sb[slot][pl.ds(offset, size)] - peak)
                    part = jnp.sum(expos, axis=0, keepdims=True)
                    prod = nn_dot(vn[row, cols, pl.ds(start, size)], expos.astype(BF))
                    total = part if total is None else total + part
                    summed = prod if summed is None else summed + prod
                    offset += size
                even, odd = summed[:HD, :BLOCK], summed[HD:, BLOCK:]
                if not first:
                    decay = jnp.exp(before - peak)
                    total = total + ls[j, pair] * decay
                    even = even + acc[j, pair, 0] * decay[:, :BLOCK]
                    odd = odd + acc[j, pair, 1] * decay[:, BLOCK:]
                ms[j, pair] = peak
                ls[j, pair] = total
                acc[j, pair, 0] = even
                acc[j, pair, 1] = odd

        pipelined(score, finish_pair)

    def far(tiles, own=False):
        whiches = []
        for i, (owner, both, one) in enumerate(tiles):
            col, which = lookup(owner, ids)
            whiches.append(which)
            rows = slice(i * BLOCK, (i + 1) * BLOCK)
            x[rows] = one[...] if both is None else jnp.where(col == 1, both[1], both[0])
        rows = pl.ds(0, len(tiles) * BLOCK)
        project(x.at[rows], kt.at[rows], vt.at[:, rows])
        if own:
            col, which = lookup(lon, ids)
            last = slice(len(tiles) * BLOCK, (len(tiles) + 1) * BLOCK)
            whiches.append(which)
            kt[last] = jnp.where(col == 1, kn[0, BLOCK : 2 * BLOCK], kn[0, :BLOCK])
            vt[:, last] = jnp.where(col == 1, vn[0, :, BLOCK : 2 * BLOCK], vn[0, :, :BLOCK])
        count = len(whiches)
        keys = count * BLOCK

        def score(pair, slot):
            cols = pair_cols(pair)
            for i in range(count):
                s = nn_dot(kt[i * BLOCK : (i + 1) * BLOCK, cols], qmt[whiches[i], pair])
                sb[slot][i * BLOCK : (i + 1) * BLOCK] = s
                pk[slot][i] = jnp.max(s, axis=0, keepdims=True)

        def finish_pair(pair, slot):
            cols = pair_cols(pair)
            peaks = [pk[slot][i] for i in range(count)]
            before = [ms[j, pair] for j in range(2)]
            now = []
            for j in range(2):
                peak = before[j]
                for i in range(count):
                    peak = jnp.maximum(peak, jnp.where(whiches[i] == j, peaks[i], before[j]))
                now.append(peak)
            decay = [jnp.exp(before[j] - now[j]) for j in range(2)]
            totals = [ls[j, pair] * decay[j] for j in range(2)]
            weights = [[], []]
            for i in range(count):
                mine = whiches[i] == 0
                expos = jnp.exp(sb[slot][i * BLOCK : (i + 1) * BLOCK] - jnp.where(mine, now[0], now[1]))
                part = jnp.sum(expos, axis=0, keepdims=True)
                rounded = expos.astype(BF)
                none = jnp.zeros_like(rounded)
                totals[0] = totals[0] + jnp.where(mine, part, 0.0)
                totals[1] = totals[1] + jnp.where(mine, 0.0, part)
                weights[0].append(jnp.where(mine, rounded, none))
                weights[1].append(jnp.where(mine, none, rounded))
            for j in range(2):
                summed = nn_dot(vt[cols, :keys], jnp.concatenate(weights[j], axis=0))
                ms[j, pair] = now[j]
                ls[j, pair] = totals[j]
                acc[j, pair, 0] = acc[j, pair, 0] * decay[j][:, :BLOCK] + summed[:HD, :BLOCK]
                acc[j, pair, 1] = acc[j, pair, 1] * decay[j][:, BLOCK:] + summed[HD:, BLOCK:]

        pipelined(score, finish_pair)

    def own_projection():
        own = g.at[lon]

        @pl.loop(0, width // 128)
        def _(step):
            cols = pl.ds(pl.multiple_of(step * 128, 128), 128)
            v_cols = pl.ds(pl.multiple_of(2 * width + step * 128, 128), 128)
            wvt[cols, :] = wq[:, v_cols].T

        @pl.loop(0, width // 256)
        def _(step):
            cols = pl.ds(pl.multiple_of(step * 256, 256), 256)
            tokens = own[...].reshape(2 * BLOCK, width)
            queries = nn_dot(tokens, wq[:, cols]).astype(BF).astype(F32) * HD**-0.5
            row = lax.broadcasted_iota(jnp.int32, (BLOCK, BLOCK), 0)
            for j in range(2):
                for half in range(2):
                    block = queries[j * BLOCK : (j + 1) * BLOCK, half * 128 : (half + 1) * 128].T
                    even = jnp.where(row < HD, block, 0.0)
                    odd = jnp.where(row < HD, 0.0, block)
                    qmt[j, step * 2 + half] = jnp.concatenate([even, odd], axis=1).astype(BF)
        x[: 2 * BLOCK] = own[...].reshape(2 * BLOCK, width)
        project(x.at[pl.ds(0, 256)], kn.at[0, pl.ds(0, 256)], vn.at[0, :, pl.ds(0, 256)])

    def finish():
        @pl.loop(0, PAIRS)
        def _(pair):
            cols = pair_cols(pair)
            for j in range(2):
                total = ls[j, pair]
                even = acc[j, pair, 0] / total[:, :BLOCK]
                odd = acc[j, pair, 1] / total[:, BLOCK:]
                out[j * BLOCK : (j + 1) * BLOCK, cols] = jnp.concatenate([even, odd], axis=0).T.astype(BF)

    def onward(owner, col, direction):
        send_g(owner, col, up if direction > 0 else down)

    def relay(step, col):
        wait_g(at(-step, 0), col)
        wait_g(at(step, 0), col)
        onward(at(-step, 0), col, 1)
        onward(at(step, 0), col, -1)

    def select(slot, owner, peer):
        if comm:
            col, _ = lookup(owner, ids_peers, peer)
            pick[slot] = jnp.where(col == 1, g[owner, 1], g[owner, 0])

    def hand(slot, dev):
        send(pick.at[slot], picked.at[slot], pick_sem.at[slot], dev)

    def given(slot):
        arrived(picked.at[slot], pick_sem.at[slot])

    def both(step, line):
        owner = at(step, line)
        return owner, g.at[owner], None

    def single(step, slot):
        return at(step, 1), None, picked.at[slot]

    for load in loads:
        load.wait()
    if compute:
        own_projection()

    chip = (lat_chip, lon)
    send(kn.at[0, pl.ds(0, 256)], kn.at[1, pl.ds(0, 256)], chip_sem.at[0], chip)
    send(vn.at[0, :, pl.ds(0, 256)], vn.at[1, :, pl.ds(0, 256)], chip_sem.at[1], chip)
    relay(1, 1)
    if comm:
        for peer in range(3):
            arrived(ids_in.at[peer], ids_sem.at[peer])
        table = pltpu.make_async_copy(ids_in, ids_peers, ids_sem.at[3])
        table.start()
        table.wait()
    arrived(kn.at[1, pl.ds(0, 256)], chip_sem.at[0])
    arrived(vn.at[1, :, pl.ds(0, 256)], chip_sem.at[1])
    if compute:
        near(lambda j: ((0, 0, 256), (1, 0, 256)), True)
    relay(1, 0)

    arrived(nb.at[pl.ds(0, 2)], n_sem.at[0])
    arrived(nb.at[2], n_sem.at[1])
    arrived(nb.at[3], n_sem.at[2])
    if compute:
        @pl.when(off_inside)
        def _():
            project(nb.reshape(4 * BLOCK, width), kn.at[2], vn.at[2])
            near(lambda j: ((2, 0, 256), (2, 256 + j * BLOCK, BLOCK)), False)

    relay(2, 1)
    relay(2, 0)
    select(0, at(-2, 0), 0)
    select(1, at(2, 0), 0)
    hand(0, across)
    hand(1, across)
    if compute:
        far([both(-1, 0), both(1, 0)], own=True)

    wait_g(partner, 0)
    wait_g(partner, 1)
    turn = 1 - 2 * y_hi
    ahead = (lat, lax.rem(z + turn + n_z, n_z) * 2 + y_hi)
    send_g(partner, 1 - y_hi, ahead)
    if compute:
        far([both(0, 1), both(-2, 0), both(2, 0)])

    last = lax.rem(z + n_z - 3 * sign, n_z) * 2 + y_hi
    beyond = (lat, lax.rem(z + n_z + sign, n_z) * 2 + y_hi)
    wait_g(at(-3, 0), 1)
    wait_g(at(3, 0), 1)
    send_g(last, 1, beyond)
    wait_g(at(-3, 0), 0)
    wait_g(at(3, 0), 0)
    send_g(last, 0, beyond)
    select(2, at(-3, 0), 0)
    select(3, at(3, 0), 0)
    select(5, partner, 1)
    select(6, partner, 2)
    hand(2, across)
    hand(3, across)
    hand(5, up)
    hand(6, down)

    given(0)
    given(1)
    if compute:
        far([both(-3, 0), both(3, 0), single(-2, 0), single(2, 1)])
    wait_g(lax.rem(z - turn + n_z, n_z) * 2 + 1 - y_hi, 1 - y_hi)
    if compute:
        x[0:128] = g[lon_left, 1]
        x[128:256] = g[lon_right, 0]
        project(x.at[pl.ds(0, 256)], kn.at[0, pl.ds(256, 256)], vn.at[0, :, pl.ds(256, 256)])
    wait_g(at(4, 0), 1)
    wait_g(at(4, 0), 0)
    select(4, at(4, 0), 0)
    send(kn.at[0, pl.ds(256, 256)], kn.at[1, pl.ds(256, 256)], chip_sem.at[2], chip)
    send(vn.at[0, :, pl.ds(256, 256)], vn.at[1, :, pl.ds(256, 256)], chip_sem.at[3], chip)
    hand(4, across)
    if compute:
        far([both(4, 0)])
    arrived(kn.at[1, pl.ds(256, 256)], chip_sem.at[2])
    arrived(vn.at[1, :, pl.ds(256, 256)], chip_sem.at[3])
    if compute:
        near(lambda j: ((0, 256 + j * BLOCK, BLOCK), (1, 256 + j * BLOCK, BLOCK)), False)
    given(5)
    given(6)
    given(2)
    given(3)
    if compute:
        far([single(-1, 5), single(1, 6), single(-3, 2), single(3, 3)])
    given(4)
    if compute:
        far([single(4, 4)])
        finish()
    else:
        out[...] = g[lon].reshape(out.shape)
    for copy in sends:
        copy.wait_send()


def on_device(tokens, w_qkv, w_out, tele_ids, comm=True, compute=True):
    shape = tokens.shape
    width = shape[3]
    tokens = tokens.reshape(2, BLOCK, width)
    n_lon = lax.axis_size("lon")
    anywhere = pl.BlockSpec(memory_space=pl.ANY)
    attended = pl.pallas_call(
        functools.partial(layer_kernel, comm, compute),
        out_shape=jax.ShapeDtypeStruct((2 * BLOCK, width), BF),
        in_specs=[pl.BlockSpec(memory_space=pltpu.SMEM)] + [anywhere] * 3,
        out_specs=pl.BlockSpec(memory_space=pltpu.VMEM),
        scratch_shapes=[
            pltpu.VMEM((n_lon, 2, BLOCK, width), BF),
            pltpu.VMEM((4, BLOCK, width), BF),
            pltpu.VMEM((7, BLOCK, width), BF),
            pltpu.VMEM((7, BLOCK, width), BF),
            pltpu.VMEM((width, 3 * width), BF),
            pltpu.VMEM((width, width), BF),
            pltpu.VMEM((4 * BLOCK, width), BF),
            pltpu.VMEM((3, 4 * BLOCK, width), BF),
            pltpu.VMEM((3, width, 4 * BLOCK), BF),
            pltpu.VMEM((4 * BLOCK, width), BF),
            pltpu.VMEM((width, 4 * BLOCK), BF),
            pltpu.VMEM((2, PAIRS, 2 * HD, 2 * BLOCK), BF),
            pltpu.VMEM((2, PAIRS, 1, 2 * BLOCK), F32),
            pltpu.VMEM((2, PAIRS, 1, 2 * BLOCK), F32),
            pltpu.VMEM((2, PAIRS, 2, HD, BLOCK), F32),
            pltpu.VMEM((8 * BLOCK, 2 * BLOCK), F32),
            pltpu.VMEM((8 * BLOCK, 2 * BLOCK), F32),
            pltpu.VMEM((4, 1, 2 * BLOCK), F32),
            pltpu.VMEM((4, 1, 2 * BLOCK), F32),
            pltpu.VMEM((3, 1, 2, TELE), jnp.int32),
            pltpu.SMEM((3, 1, 2, TELE), jnp.int32),
            pltpu.SemaphoreType.DMA((SENDS,)),
            pltpu.SemaphoreType.DMA((n_lon, 2)),
            pltpu.SemaphoreType.DMA((3,)),
            pltpu.SemaphoreType.DMA((4,)),
            pltpu.SemaphoreType.DMA((7,)),
            pltpu.SemaphoreType.DMA((4,)),
            pltpu.SemaphoreType.DMA((2,)),
        ],
        compiler_params=pltpu.CompilerParams(
            collective_id=0 if comm else None, has_side_effects=True, vmem_limit_bytes=60 * 1024 * 1024
        ),
        name="layer",
    )(tele_ids, tele_ids, tokens, w_qkv)
    mixed = jnp.dot(attended, w_out, preferred_element_type=F32).astype(BF)
    return mixed.reshape(shape)


def solution(mesh):
    return jax.shard_map(
        on_device,
        mesh=mesh,
        in_specs=(P("lat", "lon", None, None), P(), P(), P("lat", "lon", None)),
        out_specs=P("lat", "lon", None, None),
        check_vma=False,
    )
```

```python
import functools

import jax
import jax.numpy as jnp
from jax import lax
from jax.experimental import pallas as pl
from jax.experimental.pallas import tpu as pltpu
from jax.sharding import PartitionSpec as P

MESH = pl.DeviceIdType.MESH
BF = jnp.bfloat16
F32 = jnp.float32
H = 16
HD = 64
BLOCK = 128
PAIRS = H // 2
SENDS = 40
TELE = 8
UNROLL = 2
SPAN = 4


def nt_dot(a, b):
    return lax.dot_general(a, b, (((1,), (1,)), ((), ())), preferred_element_type=F32)


def nn_dot(a, b):
    return jnp.dot(a, b, preferred_element_type=F32)


def layer_kernel(
    comm,
    compute,
    ids,
    ids_hbm,
    tok,
    wqkv,
    out,
    g,
    nb,
    pick,
    picked,
    wq,
    wvt,
    x,
    kn,
    vn,
    kt,
    vt,
    qmt,
    ms,
    ls,
    acc,
    sb0,
    sb1,
    pk0,
    pk1,
    ids_in,
    ids_peers,
    send_sem,
    g_sem,
    n_sem,
    chip_sem,
    pick_sem,
    ids_sem,
    load_sem,
):
    n_lat, n_lon = lax.axis_size("lat"), lax.axis_size("lon")
    n_z = n_lon // 2
    width = wq.shape[0]
    lat, lon = lax.axis_index("lat"), lax.axis_index("lon")
    z, y_hi = lon // 2, lon % 2
    core = lat % 2
    sign = 1 - 2 * core

    def at(step, line):
        return lax.rem(z + step + n_z, n_z) * 2 + (y_hi if line == 0 else 1 - y_hi)

    partner = at(0, 1)
    sb, pk = (sb0, sb1), (pk0, pk1)
    lat_chip = lat + sign
    lat_off = lax.rem(lat + n_lat - sign, n_lat)
    lon_left, lon_right = lax.rem(lon + n_lon - 1, n_lon), lax.rem(lon + 1, n_lon)
    off_inside = jnp.where(core == 0, lat > 0, lat < n_lat - 1)

    loads = [
        pltpu.make_async_copy(tok, g.at[lon], load_sem.at[0]),
        pltpu.make_async_copy(wqkv, wq, load_sem.at[1]),
    ]
    for load in loads:
        load.start()

    sends = []

    def send(src, dst, sem, dev):
        if comm:
            copy = pltpu.make_async_remote_copy(
                src_ref=src,
                dst_ref=dst,
                send_sem=send_sem.at[len(sends)],
                recv_sem=sem,
                device_id=dev,
                device_id_type=MESH,
            )
            copy.start()
            sends.append(copy)

    def arrived(ref, sem):
        if comm:
            pltpu.make_async_remote_copy(
                src_ref=ref,
                dst_ref=ref,
                send_sem=send_sem.at[0],
                recv_sem=sem,
                device_id=(lat, partner),
                device_id_type=MESH,
            ).wait_recv()

    def send_g(owner, col, dev):
        send(g.at[owner, col], g.at[owner, col], g_sem.at[owner, col], dev)

    def wait_g(owner, col):
        arrived(g.at[owner, col], g_sem.at[owner, col])

    if comm:
        barrier = pltpu.get_barrier_semaphore()
        friends = [
            (lat, at(1, 0)),
            (lat, at(-1, 0)),
            (lat, partner),
            (lat_chip, lon),
            (lat_off, lon),
            (lat_off, lon_left),
            (lat_off, lon_right),
        ]
        for friend in friends:
            pl.semaphore_signal(barrier, inc=1, device_id=friend, device_id_type=MESH)
        pl.semaphore_wait(barrier, len(friends))

    up, down = (lat, at(1, 0)), (lat, at(-1, 0))
    across = (lat, partner)

    def send_own(col, dev):
        send(tok.at[col], g.at[lon, col], g_sem.at[lon, col], dev)

    send(ids_hbm, ids_in.at[0], ids_sem.at[0], across)
    send(ids_hbm, ids_in.at[2], ids_sem.at[2], up)
    send(ids_hbm, ids_in.at[1], ids_sem.at[1], down)
    send(tok, nb.at[pl.ds(0, 2)], n_sem.at[0], (lat_off, lon))
    send(tok.at[1], nb.at[2], n_sem.at[1], (lat_off, lon_right))
    send(tok.at[0], nb.at[3], n_sem.at[2], (lat_off, lon_left))
    send_own(1, up)
    send_own(1, down)
    send_own(0, up)
    send_own(0, down)
    send_own(0, across)
    send_own(1, across)

    def lookup(owner, table, peer=None):
        col = jnp.int32(0)
        which = jnp.int32(0)
        for entry in range(2 * TELE):
            value = table[0, entry // TELE, entry % TELE] if peer is None else table[peer, 0, entry // TELE, entry % TELE]
            hit = lax.shift_right_logical(value, 1) == owner
            col = jnp.where(hit, value & 1, col)
            which = jnp.where(hit, jnp.int32(entry // TELE), which)
        return col, which

    def project(source, k_dst, v_dst):
        @pl.loop(0, width // 256, unroll=UNROLL)
        def _(step):
            cols = pl.ds(pl.multiple_of(step * 256, 256), 256)
            k_cols = pl.ds(pl.multiple_of(width + step * 256, 256), 256)
            k_dst[:, cols] = nn_dot(source[...], wq[:, k_cols]).astype(BF)
            v_dst[cols, :] = nt_dot(wvt[cols, :], source[...]).astype(BF)

    def pair_cols(pair):
        return pl.ds(pl.multiple_of(pair * 128, 128), 128)

    def pipelined(score, finish_pair):
        score(0, 0)

        @pl.loop(0, PAIRS // SPAN)
        def _(step):
            for k in range(SPAN):
                pair = step * SPAN + k
                score(jnp.minimum(pair + 1, PAIRS - 1), (k + 1) % 2)
                finish_pair(pair, k % 2)

    def near(keys_of, first):
        sizes = [size for _, _, size in keys_of(0)]
        count = sum(sizes)

        def score(pair, slot):
            cols = pair_cols(pair)
            for j in range(2):
                queries = qmt[j, pair]
                offset = j * count
                peak = None
                for row, start, size in keys_of(j):
                    s = nn_dot(kn[row, pl.ds(start, size), cols], queries)
                    sb[slot][pl.ds(offset, size)] = s
                    top = jnp.max(s, axis=0, keepdims=True)
                    peak = top if peak is None else jnp.maximum(peak, top)
                    offset += size
                pk[slot][j] = peak

        def finish_pair(pair, slot):
            cols = pair_cols(pair)
            for j in range(2):
                peak = pk[slot][j]
                if not first:
                    before = ms[j, pair]
                    peak = jnp.maximum(peak, before)
                total = None
                summed = None
                offset = j * count
                for row, start, size in keys_of(j):
                    expos = jnp.exp(sb[slot][pl.ds(offset, size)] - peak)
                    part = jnp.sum(expos, axis=0, keepdims=True)
                    prod = nn_dot(vn[row, cols, pl.ds(start, size)], expos.astype(BF))
                    total = part if total is None else total + part
                    summed = prod if summed is None else summed + prod
                    offset += size
                even, odd = summed[:HD, :BLOCK], summed[HD:, BLOCK:]
                if not first:
                    decay = jnp.exp(before - peak)
                    total = total + ls[j, pair] * decay
                    even = even + acc[j, pair, 0] * decay[:, :BLOCK]
                    odd = odd + acc[j, pair, 1] * decay[:, BLOCK:]
                ms[j, pair] = peak
                ls[j, pair] = total
                acc[j, pair, 0] = even
                acc[j, pair, 1] = odd

        pipelined(score, finish_pair)

    def far(tiles, own=False):
        whiches = []
        for i, (owner, both, one) in enumerate(tiles):
            col, which = lookup(owner, ids)
            whiches.append(which)
            rows = slice(i * BLOCK, (i + 1) * BLOCK)
            x[rows] = one[...] if both is None else jnp.where(col == 1, both[1], both[0])
        rows = pl.ds(0, len(tiles) * BLOCK)
        project(x.at[rows], kt.at[rows], vt.at[:, rows])
        if own:
            col, which = lookup(lon, ids)
            last = slice(len(tiles) * BLOCK, (len(tiles) + 1) * BLOCK)
            whiches.append(which)
            kt[last] = jnp.where(col == 1, kn[0, BLOCK : 2 * BLOCK], kn[0, :BLOCK])
            vt[:, last] = jnp.where(col == 1, vn[0, :, BLOCK : 2 * BLOCK], vn[0, :, :BLOCK])
        count = len(whiches)
        keys = count * BLOCK

        def score(pair, slot):
            cols = pair_cols(pair)
            for i in range(count):
                s = nn_dot(kt[i * BLOCK : (i + 1) * BLOCK, cols], qmt[whiches[i], pair])
                sb[slot][i * BLOCK : (i + 1) * BLOCK] = s
                pk[slot][i] = jnp.max(s, axis=0, keepdims=True)

        def finish_pair(pair, slot):
            cols = pair_cols(pair)
            peaks = [pk[slot][i] for i in range(count)]
            before = [ms[j, pair] for j in range(2)]
            now = []
            for j in range(2):
                peak = before[j]
                for i in range(count):
                    peak = jnp.maximum(peak, jnp.where(whiches[i] == j, peaks[i], before[j]))
                now.append(peak)
            decay = [jnp.exp(before[j] - now[j]) for j in range(2)]
            totals = [ls[j, pair] * decay[j] for j in range(2)]
            weights = [[], []]
            for i in range(count):
                mine = whiches[i] == 0
                expos = jnp.exp(sb[slot][i * BLOCK : (i + 1) * BLOCK] - jnp.where(mine, now[0], now[1]))
                part = jnp.sum(expos, axis=0, keepdims=True)
                rounded = expos.astype(BF)
                none = jnp.zeros_like(rounded)
                totals[0] = totals[0] + jnp.where(mine, part, 0.0)
                totals[1] = totals[1] + jnp.where(mine, 0.0, part)
                weights[0].append(jnp.where(mine, rounded, none))
                weights[1].append(jnp.where(mine, none, rounded))
            for j in range(2):
                summed = nn_dot(vt[cols, :keys], jnp.concatenate(weights[j], axis=0))
                ms[j, pair] = now[j]
                ls[j, pair] = totals[j]
                acc[j, pair, 0] = acc[j, pair, 0] * decay[j][:, :BLOCK] + summed[:HD, :BLOCK]
                acc[j, pair, 1] = acc[j, pair, 1] * decay[j][:, BLOCK:] + summed[HD:, BLOCK:]

        pipelined(score, finish_pair)

    def own_projection():
        own = g.at[lon]

        @pl.loop(0, width // 128)
        def _(step):
            cols = pl.ds(pl.multiple_of(step * 128, 128), 128)
            v_cols = pl.ds(pl.multiple_of(2 * width + step * 128, 128), 128)
            wvt[cols, :] = wq[:, v_cols].T

        @pl.loop(0, width // 256)
        def _(step):
            cols = pl.ds(pl.multiple_of(step * 256, 256), 256)
            tokens = own[...].reshape(2 * BLOCK, width)
            queries = nn_dot(tokens, wq[:, cols]).astype(BF).astype(F32) * HD**-0.5
            row = lax.broadcasted_iota(jnp.int32, (BLOCK, BLOCK), 0)
            for j in range(2):
                for half in range(2):
                    block = queries[j * BLOCK : (j + 1) * BLOCK, half * 128 : (half + 1) * 128].T
                    even = jnp.where(row < HD, block, 0.0)
                    odd = jnp.where(row < HD, 0.0, block)
                    qmt[j, step * 2 + half] = jnp.concatenate([even, odd], axis=1).astype(BF)
        x[: 2 * BLOCK] = own[...].reshape(2 * BLOCK, width)
        project(x.at[pl.ds(0, 256)], kn.at[0, pl.ds(0, 256)], vn.at[0, :, pl.ds(0, 256)])

    def finish():
        @pl.loop(0, PAIRS)
        def _(pair):
            cols = pair_cols(pair)
            for j in range(2):
                total = ls[j, pair]
                even = acc[j, pair, 0] / total[:, :BLOCK]
                odd = acc[j, pair, 1] / total[:, BLOCK:]
                out[j * BLOCK : (j + 1) * BLOCK, cols] = jnp.concatenate([even, odd], axis=0).T.astype(BF)

    def onward(owner, col, direction):
        send_g(owner, col, up if direction > 0 else down)

    def relay(step, col):
        wait_g(at(-step, 0), col)
        wait_g(at(step, 0), col)
        onward(at(-step, 0), col, 1)
        onward(at(step, 0), col, -1)

    def select(slot, owner, peer):
        if comm:
            col, _ = lookup(owner, ids_peers, peer)
            pick[slot] = jnp.where(col == 1, g[owner, 1], g[owner, 0])

    def hand(slot, dev):
        send(pick.at[slot], picked.at[slot], pick_sem.at[slot], dev)

    def given(slot):
        arrived(picked.at[slot], pick_sem.at[slot])

    def both(step, line):
        owner = at(step, line)
        return owner, g.at[owner], None

    def single(step, slot):
        return at(step, 1), None, picked.at[slot]

    for load in loads:
        load.wait()
    if compute:
        own_projection()

    chip = (lat_chip, lon)
    send(kn.at[0, pl.ds(0, 256)], kn.at[1, pl.ds(0, 256)], chip_sem.at[0], chip)
    send(vn.at[0, :, pl.ds(0, 256)], vn.at[1, :, pl.ds(0, 256)], chip_sem.at[1], chip)
    relay(1, 1)
    if comm:
        for peer in range(3):
            arrived(ids_in.at[peer], ids_sem.at[peer])
        table = pltpu.make_async_copy(ids_in, ids_peers, ids_sem.at[3])
        table.start()
        table.wait()
    arrived(kn.at[1, pl.ds(0, 256)], chip_sem.at[0])
    arrived(vn.at[1, :, pl.ds(0, 256)], chip_sem.at[1])
    if compute:
        near(lambda j: ((0, 0, 256), (1, 0, 256)), True)
    relay(1, 0)

    arrived(nb.at[pl.ds(0, 2)], n_sem.at[0])
    arrived(nb.at[2], n_sem.at[1])
    arrived(nb.at[3], n_sem.at[2])
    if compute:
        @pl.when(off_inside)
        def _():
            project(nb.reshape(4 * BLOCK, width), kn.at[2], vn.at[2])
            near(lambda j: ((2, 0, 256), (2, 256 + j * BLOCK, BLOCK)), False)

    relay(2, 1)
    relay(2, 0)
    select(0, at(-2, 0), 0)
    select(1, at(2, 0), 0)
    hand(0, across)
    hand(1, across)
    if compute:
        far([both(-1, 0), both(1, 0)], own=True)

    wait_g(partner, 0)
    wait_g(partner, 1)
    turn = 1 - 2 * y_hi
    ahead = (lat, lax.rem(z + turn + n_z, n_z) * 2 + y_hi)
    send_g(partner, 1 - y_hi, ahead)
    if compute:
        far([both(-2, 0), both(2, 0)])
    given(0)
    if compute:
        far([both(0, 1), single(-2, 0)])

    last = lax.rem(z + n_z - 3 * sign, n_z) * 2 + y_hi
    beyond = (lat, lax.rem(z + n_z + sign, n_z) * 2 + y_hi)
    wait_g(at(-3, 0), 1)
    wait_g(at(3, 0), 1)
    send_g(last, 1, beyond)
    wait_g(at(-3, 0), 0)
    wait_g(at(3, 0), 0)
    send_g(last, 0, beyond)
    select(2, at(-3, 0), 0)
    select(3, at(3, 0), 0)
    select(5, partner, 1)
    select(6, partner, 2)
    hand(2, across)
    hand(3, across)
    hand(5, up)
    hand(6, down)

    if compute:
        far([both(-3, 0), both(3, 0)])
    wait_g(lax.rem(z - turn + n_z, n_z) * 2 + 1 - y_hi, 1 - y_hi)
    if compute:
        x[0:128] = g[lon_left, 1]
        x[128:256] = g[lon_right, 0]
        project(x.at[pl.ds(0, 256)], kn.at[0, pl.ds(256, 256)], vn.at[0, :, pl.ds(256, 256)])
    given(1)
    given(2)
    send(kn.at[0, pl.ds(256, 256)], kn.at[1, pl.ds(256, 256)], chip_sem.at[2], chip)
    send(vn.at[0, :, pl.ds(256, 256)], vn.at[1, :, pl.ds(256, 256)], chip_sem.at[3], chip)
    if compute:
        far([single(2, 1), single(-3, 2)])
    wait_g(at(4, 0), 1)
    wait_g(at(4, 0), 0)
    select(4, at(4, 0), 0)
    arrived(kn.at[1, pl.ds(256, 256)], chip_sem.at[2])
    arrived(vn.at[1, :, pl.ds(256, 256)], chip_sem.at[3])
    hand(4, across)
    if compute:
        near(lambda j: ((0, 256 + j * BLOCK, BLOCK), (1, 256 + j * BLOCK, BLOCK)), False)
    given(5)
    given(6)
    given(3)
    if compute:
        far([both(4, 0), single(-1, 5), single(1, 6), single(3, 3)])
    given(4)
    if compute:
        far([single(4, 4)])
        finish()
    else:
        out[...] = g[lon].reshape(out.shape)
    for copy in sends:
        copy.wait_send()


def on_device(tokens, w_qkv, w_out, tele_ids, comm=True, compute=True):
    shape = tokens.shape
    width = shape[3]
    tokens = tokens.reshape(2, BLOCK, width)
    n_lon = lax.axis_size("lon")
    anywhere = pl.BlockSpec(memory_space=pl.ANY)
    hbm = pltpu.with_memory_space_constraint
    attended = pl.pallas_call(
        functools.partial(layer_kernel, comm, compute),
        out_shape=jax.ShapeDtypeStruct((2 * BLOCK, width), BF),
        in_specs=[pl.BlockSpec(memory_space=pltpu.SMEM)] + [anywhere] * 3,
        out_specs=pl.BlockSpec(memory_space=pltpu.VMEM),
        scratch_shapes=[
            pltpu.VMEM((n_lon, 2, BLOCK, width), BF),
            pltpu.VMEM((4, BLOCK, width), BF),
            pltpu.VMEM((7, BLOCK, width), BF),
            pltpu.VMEM((7, BLOCK, width), BF),
            pltpu.VMEM((width, 3 * width), BF),
            pltpu.VMEM((width, width), BF),
            pltpu.VMEM((4 * BLOCK, width), BF),
            pltpu.VMEM((3, 4 * BLOCK, width), BF),
            pltpu.VMEM((3, width, 4 * BLOCK), BF),
            pltpu.VMEM((4 * BLOCK, width), BF),
            pltpu.VMEM((width, 4 * BLOCK), BF),
            pltpu.VMEM((2, PAIRS, 2 * HD, 2 * BLOCK), BF),
            pltpu.VMEM((2, PAIRS, 1, 2 * BLOCK), F32),
            pltpu.VMEM((2, PAIRS, 1, 2 * BLOCK), F32),
            pltpu.VMEM((2, PAIRS, 2, HD, BLOCK), F32),
            pltpu.VMEM((8 * BLOCK, 2 * BLOCK), F32),
            pltpu.VMEM((8 * BLOCK, 2 * BLOCK), F32),
            pltpu.VMEM((4, 1, 2 * BLOCK), F32),
            pltpu.VMEM((4, 1, 2 * BLOCK), F32),
            pltpu.VMEM((3, 1, 2, TELE), jnp.int32),
            pltpu.SMEM((3, 1, 2, TELE), jnp.int32),
            pltpu.SemaphoreType.DMA((SENDS,)),
            pltpu.SemaphoreType.DMA((n_lon, 2)),
            pltpu.SemaphoreType.DMA((3,)),
            pltpu.SemaphoreType.DMA((4,)),
            pltpu.SemaphoreType.DMA((7,)),
            pltpu.SemaphoreType.DMA((4,)),
            pltpu.SemaphoreType.DMA((2,)),
        ],
        compiler_params=pltpu.CompilerParams(
            collective_id=0 if comm else None, has_side_effects=True, vmem_limit_bytes=44 * 1024 * 1024
        ),
        name="layer",
    )(tele_ids, hbm(tele_ids, pltpu.HBM), hbm(tokens, pltpu.HBM), hbm(w_qkv, pltpu.HBM))
    mixed = jnp.dot(attended, w_out, preferred_element_type=F32).astype(BF)
    return mixed.reshape(shape)


def solution(mesh):
    return jax.shard_map(
        on_device,
        mesh=mesh,
        in_specs=(P("lat", "lon", None, None), P(), P(), P("lat", "lon", None)),
        out_specs=P("lat", "lon", None, None),
        check_vma=False,
    )
```

```python
import functools

import jax
import jax.numpy as jnp
from jax import lax
from jax.experimental import pallas as pl
from jax.experimental.pallas import tpu as pltpu
from jax.sharding import PartitionSpec as P

MESH = pl.DeviceIdType.MESH
BF = jnp.bfloat16
F32 = jnp.float32
H = 16
HD = 64
BLOCK = 128
PAIRS = H // 2
SENDS = 40
TELE = 8
UNROLL = 2
SPAN = 4


def nt_dot(a, b):
    return lax.dot_general(a, b, (((1,), (1,)), ((), ())), preferred_element_type=F32)


def nn_dot(a, b):
    return jnp.dot(a, b, preferred_element_type=F32)


def layer_kernel(
    comm,
    compute,
    ids,
    ids_hbm,
    tok,
    wqkv,
    out,
    g,
    nb,
    pick,
    picked,
    wq,
    wvt,
    x,
    kn,
    vn,
    kt,
    vt,
    qmt,
    ms,
    ls,
    acc,
    sb0,
    sb1,
    pk0,
    pk1,
    ids_in,
    ids_peers,
    send_sem,
    g_sem,
    n_sem,
    chip_sem,
    pick_sem,
    ids_sem,
    load_sem,
):
    n_lat, n_lon = lax.axis_size("lat"), lax.axis_size("lon")
    n_z = n_lon // 2
    width = wq.shape[0]
    lat, lon = lax.axis_index("lat"), lax.axis_index("lon")
    z, y_hi = lon // 2, lon % 2
    core = lat % 2
    sign = 1 - 2 * core

    def at(step, line):
        return lax.rem(z + step + n_z, n_z) * 2 + (y_hi if line == 0 else 1 - y_hi)

    partner = at(0, 1)
    sb, pk = (sb0, sb1), (pk0, pk1)
    lat_chip = lat + sign
    lat_off = lax.rem(lat + n_lat - sign, n_lat)
    lon_left, lon_right = lax.rem(lon + n_lon - 1, n_lon), lax.rem(lon + 1, n_lon)
    off_inside = jnp.where(core == 0, lat > 0, lat < n_lat - 1)

    loads = [
        pltpu.make_async_copy(tok, g.at[lon], load_sem.at[0]),
        pltpu.make_async_copy(wqkv, wq, load_sem.at[1]),
    ]
    for load in loads:
        load.start()

    sends = []

    def send(src, dst, sem, dev):
        if comm:
            copy = pltpu.make_async_remote_copy(
                src_ref=src,
                dst_ref=dst,
                send_sem=send_sem.at[len(sends)],
                recv_sem=sem,
                device_id=dev,
                device_id_type=MESH,
            )
            copy.start()
            sends.append(copy)

    def arrived(ref, sem):
        if comm:
            pltpu.make_async_remote_copy(
                src_ref=ref,
                dst_ref=ref,
                send_sem=send_sem.at[0],
                recv_sem=sem,
                device_id=(lat, partner),
                device_id_type=MESH,
            ).wait_recv()

    def send_g(owner, col, dev):
        send(g.at[owner, col], g.at[owner, col], g_sem.at[owner, col], dev)

    def wait_g(owner, col):
        arrived(g.at[owner, col], g_sem.at[owner, col])

    if comm:
        barrier = pltpu.get_barrier_semaphore()
        friends = [
            (lat, at(1, 0)),
            (lat, at(-1, 0)),
            (lat, partner),
            (lat_chip, lon),
            (lat_off, lon),
            (lat_off, lon_left),
            (lat_off, lon_right),
        ]
        for friend in friends:
            pl.semaphore_signal(barrier, inc=1, device_id=friend, device_id_type=MESH)
        pl.semaphore_wait(barrier, len(friends))

    up, down = (lat, at(1, 0)), (lat, at(-1, 0))
    across = (lat, partner)

    def send_own(col, dev):
        send(tok.at[col], g.at[lon, col], g_sem.at[lon, col], dev)

    send(ids_hbm, ids_in.at[0], ids_sem.at[0], across)
    send(ids_hbm, ids_in.at[2], ids_sem.at[2], up)
    send(ids_hbm, ids_in.at[1], ids_sem.at[1], down)
    send(tok, nb.at[pl.ds(0, 2)], n_sem.at[0], (lat_off, lon))
    send(tok.at[1], nb.at[2], n_sem.at[1], (lat_off, lon_right))
    send(tok.at[0], nb.at[3], n_sem.at[2], (lat_off, lon_left))
    send_own(1, up)
    send_own(1, down)
    send_own(0, up)
    send_own(0, down)
    send_own(0, across)
    send_own(1, across)

    def lookup(owner, table, peer=None):
        col = jnp.int32(0)
        which = jnp.int32(0)
        for entry in range(2 * TELE):
            value = table[0, entry // TELE, entry % TELE] if peer is None else table[peer, 0, entry // TELE, entry % TELE]
            hit = lax.shift_right_logical(value, 1) == owner
            col = jnp.where(hit, value & 1, col)
            which = jnp.where(hit, jnp.int32(entry // TELE), which)
        return col, which

    def project(source, k_dst, v_dst):
        @pl.loop(0, width // 256, unroll=UNROLL)
        def _(step):
            cols = pl.ds(pl.multiple_of(step * 256, 256), 256)
            k_cols = pl.ds(pl.multiple_of(width + step * 256, 256), 256)
            k_dst[:, cols] = nn_dot(source[...], wq[:, k_cols]).astype(BF)
            v_dst[cols, :] = nt_dot(wvt[cols, :], source[...]).astype(BF)

    def pair_cols(pair):
        return pl.ds(pl.multiple_of(pair * 128, 128), 128)

    def pipelined(score, finish_pair):
        score(0, 0)

        @pl.loop(0, PAIRS // SPAN)
        def _(step):
            for k in range(SPAN):
                pair = step * SPAN + k
                score(jnp.minimum(pair + 1, PAIRS - 1), (k + 1) % 2)
                finish_pair(pair, k % 2)

    def together(score, finish_pair):
        @pl.loop(0, PAIRS // SPAN)
        def _(step):
            for k in range(SPAN):
                score(step * SPAN + k, k)
            for k in range(SPAN):
                finish_pair(step * SPAN + k, k)

    def near(keys_of, first):
        sizes = [size for _, _, size in keys_of(0)]
        count = sum(sizes)

        def score(pair, slot):
            cols = pair_cols(pair)
            for j in range(2):
                queries = qmt[j, pair]
                offset = j * count
                peak = None
                for row, start, size in keys_of(j):
                    s = nn_dot(kn[row, pl.ds(start, size), cols], queries)
                    sb[slot][pl.ds(offset, size)] = s
                    top = jnp.max(s, axis=0, keepdims=True)
                    peak = top if peak is None else jnp.maximum(peak, top)
                    offset += size
                pk[slot][j] = peak

        def finish_pair(pair, slot):
            cols = pair_cols(pair)
            for j in range(2):
                peak = pk[slot][j]
                if not first:
                    before = ms[j, pair]
                    peak = jnp.maximum(peak, before)
                summed = None
                offset = j * count
                for row, start, size in keys_of(j):
                    expos = jnp.exp(sb[slot][pl.ds(offset, size)] - peak)
                    values = jnp.concatenate([vn[row, cols, pl.ds(start, size)], jnp.ones((16, size), BF)], axis=0)
                    prod = nn_dot(values, expos.astype(BF))
                    summed = prod if summed is None else summed + prod
                    offset += size
                total = summed[BLOCK : BLOCK + 1]
                even, odd = summed[:HD, :BLOCK], summed[HD:BLOCK, BLOCK:]
                if not first:
                    decay = jnp.exp(before - peak)
                    total = total + ls[j, pair] * decay
                    even = even + acc[j, pair, 0] * decay[:, :BLOCK]
                    odd = odd + acc[j, pair, 1] * decay[:, BLOCK:]
                ms[j, pair] = peak
                ls[j, pair] = total
                acc[j, pair, 0] = even
                acc[j, pair, 1] = odd

        pipelined(score, finish_pair)

    def far(tiles, own=False):
        whiches = []
        for i, (owner, both, one) in enumerate(tiles):
            col, which = lookup(owner, ids)
            whiches.append(which)
            rows = slice(i * BLOCK, (i + 1) * BLOCK)
            x[rows] = one[...] if both is None else jnp.where(col == 1, both[1], both[0])
        rows = pl.ds(0, len(tiles) * BLOCK)
        project(x.at[rows], kt.at[rows], vt.at[:, rows])
        if own:
            col, which = lookup(lon, ids)
            last = slice(len(tiles) * BLOCK, (len(tiles) + 1) * BLOCK)
            whiches.append(which)
            kt[last] = jnp.where(col == 1, kn[0, BLOCK : 2 * BLOCK], kn[0, :BLOCK])
            vt[:, last] = jnp.where(col == 1, vn[0, :, BLOCK : 2 * BLOCK], vn[0, :, :BLOCK])
        count = len(whiches)
        keys = count * BLOCK

        def base(slot):
            return slot // 2 * 4 * BLOCK

        def score(pair, slot):
            cols = pair_cols(pair)
            for i in range(count):
                s = nn_dot(kt[i * BLOCK : (i + 1) * BLOCK, cols], qmt[whiches[i], pair])
                sb[slot % 2][base(slot) + i * BLOCK : base(slot) + (i + 1) * BLOCK] = s
                pk[slot % 2][slot // 2 * 2 + i] = jnp.max(s, axis=0, keepdims=True)

        def finish_pair(pair, slot):
            cols = pair_cols(pair)
            peaks = [pk[slot % 2][slot // 2 * 2 + i] for i in range(count)]
            before = [ms[j, pair] for j in range(2)]
            now = []
            for j in range(2):
                peak = before[j]
                for i in range(count):
                    peak = jnp.maximum(peak, jnp.where(whiches[i] == j, peaks[i], before[j]))
                now.append(peak)
            decay = [jnp.exp(before[j] - now[j]) for j in range(2)]
            totals = [ls[j, pair] * decay[j] for j in range(2)]
            weights = [[], []]
            for i in range(count):
                mine = whiches[i] == 0
                expos = jnp.exp(sb[slot % 2][base(slot) + i * BLOCK : base(slot) + (i + 1) * BLOCK] - jnp.where(mine, now[0], now[1]))
                part = jnp.sum(expos, axis=0, keepdims=True)
                rounded = expos.astype(BF)
                none = jnp.zeros_like(rounded)
                totals[0] = totals[0] + jnp.where(mine, part, 0.0)
                totals[1] = totals[1] + jnp.where(mine, 0.0, part)
                weights[0].append(jnp.where(mine, rounded, none))
                weights[1].append(jnp.where(mine, none, rounded))
            for j in range(2):
                summed = nn_dot(vt[cols, :keys], jnp.concatenate(weights[j], axis=0))
                ms[j, pair] = now[j]
                ls[j, pair] = totals[j]
                acc[j, pair, 0] = acc[j, pair, 0] * decay[j][:, :BLOCK] + summed[:HD, :BLOCK]
                acc[j, pair, 1] = acc[j, pair, 1] * decay[j][:, BLOCK:] + summed[HD:, BLOCK:]

        if count <= 2:
            together(score, finish_pair)
        else:
            pipelined(score, finish_pair)

    def own_projection():
        own = g.at[lon]

        @pl.loop(0, width // 128)
        def _(step):
            cols = pl.ds(pl.multiple_of(step * 128, 128), 128)
            v_cols = pl.ds(pl.multiple_of(2 * width + step * 128, 128), 128)
            wvt[cols, :] = wq[:, v_cols].T

        @pl.loop(0, width // 256)
        def _(step):
            cols = pl.ds(pl.multiple_of(step * 256, 256), 256)
            tokens = own[...].reshape(2 * BLOCK, width)
            queries = nn_dot(tokens, wq[:, cols]).astype(BF).astype(F32) * HD**-0.5
            row = lax.broadcasted_iota(jnp.int32, (BLOCK, BLOCK), 0)
            for j in range(2):
                for half in range(2):
                    block = queries[j * BLOCK : (j + 1) * BLOCK, half * 128 : (half + 1) * 128].T
                    even = jnp.where(row < HD, block, 0.0)
                    odd = jnp.where(row < HD, 0.0, block)
                    qmt[j, step * 2 + half] = jnp.concatenate([even, odd], axis=1).astype(BF)
        x[: 2 * BLOCK] = own[...].reshape(2 * BLOCK, width)
        project(x.at[pl.ds(0, 256)], kn.at[0, pl.ds(0, 256)], vn.at[0, :, pl.ds(0, 256)])

    def finish():
        @pl.loop(0, PAIRS)
        def _(pair):
            cols = pair_cols(pair)
            for j in range(2):
                total = ls[j, pair]
                even = acc[j, pair, 0] / total[:, :BLOCK]
                odd = acc[j, pair, 1] / total[:, BLOCK:]
                out[j * BLOCK : (j + 1) * BLOCK, cols] = jnp.concatenate([even, odd], axis=0).T.astype(BF)

    def onward(owner, col, direction):
        send_g(owner, col, up if direction > 0 else down)

    def relay(step, col):
        wait_g(at(-step, 0), col)
        wait_g(at(step, 0), col)
        onward(at(-step, 0), col, 1)
        onward(at(step, 0), col, -1)

    def select(slot, owner, peer):
        if comm:
            col, _ = lookup(owner, ids_peers, peer)
            pick[slot] = jnp.where(col == 1, g[owner, 1], g[owner, 0])

    def hand(slot, dev):
        send(pick.at[slot], picked.at[slot], pick_sem.at[slot], dev)

    def given(slot):
        arrived(picked.at[slot], pick_sem.at[slot])

    def both(step, line):
        owner = at(step, line)
        return owner, g.at[owner], None

    def single(step, slot):
        return at(step, 1), None, picked.at[slot]

    for load in loads:
        load.wait()
    if compute:
        own_projection()

    chip = (lat_chip, lon)
    send(kn.at[0, pl.ds(0, 256)], kn.at[1, pl.ds(0, 256)], chip_sem.at[0], chip)
    send(vn.at[0, :, pl.ds(0, 256)], vn.at[1, :, pl.ds(0, 256)], chip_sem.at[1], chip)
    relay(1, 1)
    if comm:
        for peer in range(3):
            arrived(ids_in.at[peer], ids_sem.at[peer])
        table = pltpu.make_async_copy(ids_in, ids_peers, ids_sem.at[3])
        table.start()
        table.wait()
    arrived(kn.at[1, pl.ds(0, 256)], chip_sem.at[0])
    arrived(vn.at[1, :, pl.ds(0, 256)], chip_sem.at[1])
    if compute:
        near(lambda j: ((0, 0, 256), (1, 0, 256)), True)
    relay(1, 0)

    arrived(nb.at[pl.ds(0, 2)], n_sem.at[0])
    arrived(nb.at[2], n_sem.at[1])
    arrived(nb.at[3], n_sem.at[2])
    if compute:
        @pl.when(off_inside)
        def _():
            project(nb.reshape(4 * BLOCK, width), kn.at[2], vn.at[2])
            near(lambda j: ((2, 0, 256), (2, 256 + j * BLOCK, BLOCK)), False)

    relay(2, 1)
    relay(2, 0)
    select(0, at(-2, 0), 0)
    select(1, at(2, 0), 0)
    hand(0, across)
    hand(1, across)
    if compute:
        far([both(-1, 0), both(1, 0)], own=True)

    wait_g(partner, 0)
    wait_g(partner, 1)
    turn = 1 - 2 * y_hi
    ahead = (lat, lax.rem(z + turn + n_z, n_z) * 2 + y_hi)
    send_g(partner, 1 - y_hi, ahead)
    if compute:
        far([both(-2, 0), both(2, 0)])
    given(0)
    if compute:
        far([both(0, 1), single(-2, 0)])

    last = lax.rem(z + n_z - 3 * sign, n_z) * 2 + y_hi
    beyond = (lat, lax.rem(z + n_z + sign, n_z) * 2 + y_hi)
    wait_g(at(-3, 0), 1)
    wait_g(at(3, 0), 1)
    send_g(last, 1, beyond)
    wait_g(at(-3, 0), 0)
    wait_g(at(3, 0), 0)
    send_g(last, 0, beyond)
    select(2, at(-3, 0), 0)
    select(3, at(3, 0), 0)
    select(5, partner, 1)
    select(6, partner, 2)
    hand(2, across)
    hand(3, across)
    hand(5, up)
    hand(6, down)

    if compute:
        far([both(-3, 0), both(3, 0)])
    wait_g(lax.rem(z - turn + n_z, n_z) * 2 + 1 - y_hi, 1 - y_hi)
    if compute:
        x[0:128] = g[lon_left, 1]
        x[128:256] = g[lon_right, 0]
        project(x.at[pl.ds(0, 256)], kn.at[0, pl.ds(256, 256)], vn.at[0, :, pl.ds(256, 256)])
    given(1)
    given(2)
    send(kn.at[0, pl.ds(256, 256)], kn.at[1, pl.ds(256, 256)], chip_sem.at[2], chip)
    send(vn.at[0, :, pl.ds(256, 256)], vn.at[1, :, pl.ds(256, 256)], chip_sem.at[3], chip)
    if compute:
        far([single(2, 1), single(-3, 2)])
    wait_g(at(4, 0), 1)
    wait_g(at(4, 0), 0)
    select(4, at(4, 0), 0)
    arrived(kn.at[1, pl.ds(256, 256)], chip_sem.at[2])
    arrived(vn.at[1, :, pl.ds(256, 256)], chip_sem.at[3])
    hand(4, across)
    if compute:
        near(lambda j: ((0, 256 + j * BLOCK, BLOCK), (1, 256 + j * BLOCK, BLOCK)), False)
    given(3)
    if compute:
        far([both(4, 0), single(3, 3)])
    given(5)
    given(6)
    if compute:
        far([single(-1, 5), single(1, 6)])
    given(4)
    if compute:
        far([single(4, 4)])
        finish()
    else:
        out[...] = g[lon].reshape(out.shape)
    for copy in sends:
        copy.wait_send()


def on_device(tokens, w_qkv, w_out, tele_ids, comm=True, compute=True):
    shape = tokens.shape
    width = shape[3]
    tokens = tokens.reshape(2, BLOCK, width)
    n_lon = lax.axis_size("lon")
    anywhere = pl.BlockSpec(memory_space=pl.ANY)
    hbm = pltpu.with_memory_space_constraint
    attended = pl.pallas_call(
        functools.partial(layer_kernel, comm, compute),
        out_shape=jax.ShapeDtypeStruct((2 * BLOCK, width), BF),
        in_specs=[pl.BlockSpec(memory_space=pltpu.SMEM)] + [anywhere] * 3,
        out_specs=pl.BlockSpec(memory_space=pltpu.VMEM),
        scratch_shapes=[
            pltpu.VMEM((n_lon, 2, BLOCK, width), BF),
            pltpu.VMEM((4, BLOCK, width), BF),
            pltpu.VMEM((7, BLOCK, width), BF),
            pltpu.VMEM((7, BLOCK, width), BF),
            pltpu.VMEM((width, 3 * width), BF),
            pltpu.VMEM((width, width), BF),
            pltpu.VMEM((4 * BLOCK, width), BF),
            pltpu.VMEM((3, 4 * BLOCK, width), BF),
            pltpu.VMEM((3, width, 4 * BLOCK), BF),
            pltpu.VMEM((4 * BLOCK, width), BF),
            pltpu.VMEM((width, 4 * BLOCK), BF),
            pltpu.VMEM((2, PAIRS, 2 * HD, 2 * BLOCK), BF),
            pltpu.VMEM((2, PAIRS, 1, 2 * BLOCK), F32),
            pltpu.VMEM((2, PAIRS, 1, 2 * BLOCK), F32),
            pltpu.VMEM((2, PAIRS, 2, HD, BLOCK), F32),
            pltpu.VMEM((8 * BLOCK, 2 * BLOCK), F32),
            pltpu.VMEM((8 * BLOCK, 2 * BLOCK), F32),
            pltpu.VMEM((4, 1, 2 * BLOCK), F32),
            pltpu.VMEM((4, 1, 2 * BLOCK), F32),
            pltpu.VMEM((3, 1, 2, TELE), jnp.int32),
            pltpu.SMEM((3, 1, 2, TELE), jnp.int32),
            pltpu.SemaphoreType.DMA((SENDS,)),
            pltpu.SemaphoreType.DMA((n_lon, 2)),
            pltpu.SemaphoreType.DMA((3,)),
            pltpu.SemaphoreType.DMA((4,)),
            pltpu.SemaphoreType.DMA((7,)),
            pltpu.SemaphoreType.DMA((4,)),
            pltpu.SemaphoreType.DMA((2,)),
        ],
        compiler_params=pltpu.CompilerParams(
            collective_id=0 if comm else None, has_side_effects=True, vmem_limit_bytes=44 * 1024 * 1024
        ),
        name="layer",
    )(tele_ids, hbm(tele_ids, pltpu.HBM), hbm(tokens, pltpu.HBM), hbm(w_qkv, pltpu.HBM))
    mixed = jnp.dot(attended, w_out, preferred_element_type=F32).astype(BF)
    return mixed.reshape(shape)


def solution(mesh):
    return jax.shard_map(
        on_device,
        mesh=mesh,
        in_specs=(P("lat", "lon", None, None), P(), P(), P("lat", "lon", None)),
        out_specs=P("lat", "lon", None, None),
        check_vma=False,
    )
```
